512 devices in a mesh: sub: 64 (over z_hi, x, y, core), chan: 8 (over z_lo).
Axes of the slice: x: 4, y: 4, z: 16 (z_hi: 2, z_lo: 8; z = z_hi * 8 + z_lo), core: 2. Of those that a mesh axis runs over, the one named last changes fastest.
Arguments:
- raw_pulses: bfloat16 [2, 2048, 8, 2048], P(None, 'sub', 'chan'), may hold values from -6 to 6
- range_filter: bfloat16 [2, 2048, 1024], P(None, ('sub', 'chan')), may hold values from -0.09375 to 0.09375
- channel_mix: float32 [2, 32, 8, 8], replicated, may hold values from -1.5 to 1.5
- steer_angles: float32 [256], replicated, may hold values from -3.140625 to 3.140625
- band_offsets: int32 [4, 512], replicated, may hold values from 0 to 248
- band_weights: float32 [4, 2, 2, 512, 8], replicated, may hold values from -1 to 1
- smoothing: float32 [16384], P('sub'), may hold values from 0.3 to 0.5
Outputs:
- despeckled: float32 [16384, 1024], P('sub', 'chan')
The draws below stay inside these ranges and needn't reach their ends.
All inputs are finite; a program needn't handle non-finite values.
Results may differ from the reference program's by a relative error of at most 0.0036.
Values may be sent and summed in bfloat16 or wider, within the bound.
No kernel may reach another device: no remote copies, remote signals or barrier semaphores. Data moves between devices by JAX's collectives and lax.ppermute only.
A program may use at most 64 MiB of HBM per device.

```python
import jax
import jax.numpy as jnp
import numpy as np
from jax import lax

P_DEV = 32
SAMPLES = 2048
BINS = 1024
ANG = 256
BAND = 8
LEVELS = 4
PASSES = 3
CHANNELS = 8
PULSES = 2048
ANGLES = 16384
N_SUB = 64


def set_ends(entries, key, least, top_value):
    index_at = [jax.random.randint(jax.random.fold_in(key, axis), (), 0, length) for axis, length in enumerate(entries.shape)]
    main_axis = entries.shape.index(max(entries.shape))
    next_to = index_at[:main_axis] + [(index_at[main_axis] + 1) % entries.shape[main_axis]] + index_at[main_axis + 1:]
    return entries.at[tuple(index_at)].set(least).at[tuple(next_to)].set(top_value)


def level_of(own_key, extent, split, least, top_value):
    factor_of = 1.0
    for dim, parts in split:
        steps = jax.random.uniform(jax.random.fold_in(jax.random.fold_in(own_key, 6), dim), (parts,), jnp.float32, least / len(split), top_value / len(split))
        factor_of = factor_of * jnp.repeat(jnp.exp(steps), extent[dim] // parts).reshape((-1,) + (1,) * (len(extent) - 1 - dim))
    return factor_of


def scatter_about(own_key, extent, deviation, most, split=(), kind=jnp.bfloat16):
    loudness = level_of(own_key, extent, split, -0.22, 0.18) if split else 1.0
    values = jax.random.normal(own_key, extent, jnp.float32) * deviation * loudness
    return jnp.minimum(jnp.maximum(values, -most), most).astype(kind)


def setup_inputs(seed: int = 0) -> dict:
    keys = jax.random.split(jax.random.key(seed), 8)
    return {
        "raw_pulses": scatter_about(keys[0], (2, PULSES, CHANNELS, SAMPLES), 1.0, 6.0, ((1, 64), (2, 8))),
        "range_filter": scatter_about(keys[1], (2, SAMPLES, BINS), (2 * SAMPLES) ** -0.5, 0.09375, ((1, 512),)),
        "channel_mix": scatter_about(keys[2], (2, P_DEV, CHANNELS, CHANNELS), (2 * CHANNELS) ** -0.5, 1.5, (), jnp.float32),
        "steer_angles": jnp.clip(jax.random.uniform(keys[3], (ANG,), jnp.float32, -3.140625, 3.140625), -3.140625, 3.140625),
        "band_offsets": set_ends(jax.random.randint(keys[4], (LEVELS, 2 * ANG), 0, ANG - BAND + 1), jax.random.fold_in(keys[4], 1), 0, ANG - BAND).astype(jnp.int32),
        "band_weights": scatter_about(keys[5], (LEVELS, 2, 2, 2 * ANG, BAND), (4 * BAND) ** -0.5, 1.0, (), jnp.float32),
        "smoothing": jnp.clip(0.3 + 0.19999999 * jax.random.uniform(keys[6], (ANGLES,), jnp.float32) ** level_of(keys[6], (ANGLES,), ((0, 64),), -0.2, 0.2), 0.3, 0.5),
    }


HIGH = lax.Precision.HIGHEST

def doppler_table(count):
    index_row = jnp.arange(count, dtype=jnp.int32)
    product = index_row[:, None] * index_row[None, :] % count
    phase = 2.0 * np.pi / count * product.astype(jnp.float32)
    factor = 1.0 / np.sqrt(count)
    return ((jnp.cos(phase) * factor).astype(jnp.bfloat16), (-jnp.sin(phase) * factor).astype(jnp.bfloat16))

def steer_table(steer_angles, count):
    offsets = jnp.arange(count, dtype=jnp.int32).astype(jnp.float32) - 0.5 * count
    phase = steer_angles[:, None] * offsets[None, :]
    factor = 1.0 / np.sqrt(count)
    return ((jnp.cos(phase) * factor).astype(jnp.bfloat16), (jnp.sin(phase) * factor).astype(jnp.bfloat16))

def low_dot(left, right):
    return jnp.dot(left, right, preferred_element_type=jnp.float32)

def range_terms(echo_rows, filter_rows):
    real_part = low_dot(echo_rows[0], filter_rows[0]) - low_dot(echo_rows[1], filter_rows[1])
    imag_part = low_dot(echo_rows[0], filter_rows[1]) + low_dot(echo_rows[1], filter_rows[0])
    return jnp.stack([real_part, imag_part])

def form_image(compressed, dop_real, dop_imag, channel_mix, beam_real, beam_imag):
    pulse_count = compressed.shape[1]
    channels = compressed.shape[2]
    cells = compressed.shape[3]
    flat = compressed.reshape(2, pulse_count, channels * cells)
    spec_real = (low_dot(dop_real, flat[0]) - low_dot(dop_imag, flat[1])).reshape(pulse_count, channels, cells)
    spec_imag = (low_dot(dop_real, flat[1]) + low_dot(dop_imag, flat[0])).reshape(pulse_count, channels, cells)
    mix_real = jnp.einsum('fkc,fcb->kfb', channel_mix[0], spec_real, precision=HIGH) - jnp.einsum('fkc,fcb->kfb', channel_mix[1], spec_imag, precision=HIGH)
    mix_imag = jnp.einsum('fkc,fcb->kfb', channel_mix[0], spec_imag, precision=HIGH) + jnp.einsum('fkc,fcb->kfb', channel_mix[1], spec_real, precision=HIGH)
    recon = jnp.stack([mix_real, mix_imag]).astype(jnp.bfloat16).reshape(2, channels * pulse_count, cells)
    image_real = low_dot(beam_real, recon[0]) - low_dot(beam_imag, recon[1])
    image_imag = low_dot(beam_real, recon[1]) + low_dot(beam_imag, recon[0])
    return jnp.stack([image_real, image_imag])

def band_matrix(offsets, weights, count):
    band_width = weights.shape[-1]
    columns = jnp.arange(count, dtype=jnp.int32)
    stepping = jnp.arange(band_width, dtype=jnp.int32)
    target = offsets.astype(jnp.int32)[:, None, None] + stepping[None, :, None]
    hitting = (columns[None, None, :] == target).astype(jnp.float32)
    return jnp.einsum('crkj,kja->crka', weights, hitting, precision=HIGH)

def batched_apply(matrices, field):
    real_part = jnp.einsum('dka,dab->dkb', matrices[0], field[:, 0], precision=HIGH) - jnp.einsum('dka,dab->dkb', matrices[1], field[:, 1], precision=HIGH)
    imag_part = jnp.einsum('dka,dab->dkb', matrices[0], field[:, 1], precision=HIGH) + jnp.einsum('dka,dab->dkb', matrices[1], field[:, 0], precision=HIGH)
    return jnp.stack([real_part, imag_part], axis=1)

def reference(raw_pulses, range_filter, channel_mix, steer_angles, band_offsets, band_weights, smoothing):
    channels = raw_pulses.shape[2]
    blocks = jnp.moveaxis(raw_pulses.reshape(2, N_SUB, P_DEV, channels, SAMPLES), 1, 0)
    dop_real, dop_imag = doppler_table(P_DEV)
    beam_real, beam_imag = steer_table(steer_angles, channels * P_DEV)

    def one_block(block):
        echo_rows = block.reshape(2, P_DEV * channels, SAMPLES)
        compressed = range_terms(echo_rows, range_filter).astype(jnp.bfloat16).reshape(2, P_DEV, channels, BINS)
        return form_image(compressed, dop_real, dop_imag, channel_mix, beam_real, beam_imag)
    images = lax.map(one_block, blocks)
    index_all = np.arange(N_SUB)
    for merge_level in range(LEVELS):
        bit_value = 1 << merge_level
        lower_index = index_all & ~bit_value
        upper_index = index_all | bit_value
        half_index = index_all >> merge_level & 1
        full_band = band_matrix(band_offsets[merge_level], band_weights[merge_level], ANG)
        full_band = full_band.reshape(2, 2, 2, ANG, ANG)
        chosen = full_band[:, :, half_index]
        images = batched_apply(chosen[0], images[lower_index]) + batched_apply(chosen[1], images[upper_index])
    power = images[:, 0] * images[:, 0] + images[:, 1] * images[:, 1]
    power = power.reshape(N_SUB * ANG, BINS)
    rate = smoothing[:, None]
    for sweep in range(PASSES):
        padded = jnp.pad(power, ((0, 0), (1, 1)))
        power = power + rate * (padded[:, :-2] - 2.0 * power + padded[:, 2:])
    return power
```

```python
import functools

import jax
import jax.numpy as jnp
import ml_dtypes
import numpy as np
from jax import lax
from jax.experimental import pallas as pl
from jax.experimental.pallas import tpu as pltpu
from jax.sharding import Mesh
from jax.sharding import PartitionSpec as P

ANG = 256
BAND = 8
LEVELS = 4
PASSES = 3
PULSES = 32
CHAN = 8
GROUP = 16
ROW = 8
CUT = 9
PAD = 16
HALO = 8
COLS = GROUP * CUT
AXES = ("zh", "x1", "x0", "y", "core", "chan")
SUB = ("zh", "x1", "x0", "y", "core")
ALONG_Z = ("zh", "chan")
PLANE = ("x1", "x0", "y", "core")
MERGE = ("x0", "y", "core")
BF = jnp.bfloat16
F32 = jnp.float32
WHOLE = pl.BlockSpec(memory_space=pltpu.VMEM)
SCALAR = pl.BlockSpec(memory_space=pltpu.SMEM)


def params(mib):
    return pltpu.CompilerParams(vmem_limit_bytes=mib << 20)


def iota(shape, dim):
    return lax.broadcasted_iota(jnp.int32, shape, dim)


def dot(left, right):
    return jnp.dot(left, right, preferred_element_type=F32)


def dot_t(left, right):
    return lax.dot_general(left, right, (((1,), (1,)), ((), ())), preferred_element_type=F32)


def raw_body(raw_ref, out_ref):
    row, col = iota((512, 512), 0), iota((512, 512), 1)
    quarter, part, half, k = col >> 7, (col >> 6) & 1, (col >> 5) & 1, col & 31
    source = part * 256 + half * 128 + quarter * 32 + k
    sign = jnp.where(part == 1, -1.0, 1.0)
    order = jnp.where(row == source, sign, 0.0).astype(BF)
    rows = []
    for u in range(8):
        rows.append(
            jnp.concatenate(
                [
                    raw_ref[part, :, half * 1024 + u * 128 : half * 1024 + (u + 1) * 128]
                    for part in range(2)
                    for half in range(2)
                ],
                axis=1,
            )
        )
    moved = dot(jnp.concatenate(rows, axis=0), order).astype(BF)
    for u in range(8):
        out_ref[:, u * 512 : (u + 1) * 512] = moved[u * 32 : (u + 1) * 32]


def pick_body(filter_ref, out_ref):
    i, k = iota((128, 128), 0), iota((128, 128), 1)
    source = (((i >> 5) & 1) * 8 + ((i >> 2) & 7)) * 8 + (i >> 6) * 4 + (i & 3)
    rows = dot(jnp.where(k == source, 1.0, 0.0).astype(BF), filter_ref[...]).astype(BF)
    bins = iota((COLS, 1024), 1)
    r = iota((COLS, 1024), 0)
    dest = r // CUT
    first = 128 * (dest & 7) - HALO + 8 * CUT * (dest >> 3) + r - dest * CUT
    for g in range(ROW):
        pick = jnp.where(bins == first + CUT * g, 1.0, 0.0).astype(BF)
        block = dot_t(pick, rows).astype(BF)
        for x in range(4):
            out_ref[x, g] = block


def compress_body(filter_ref, own_ref, other_ref, out_ref):
    first, second = [], []
    for s in range(32):
        block = filter_ref[s]
        first.append(block)
        second.append(jnp.concatenate([block[:, 64:], -block[:, :64]], axis=1))
    left = jnp.concatenate(
        [jnp.concatenate(first, axis=1), jnp.concatenate(second, axis=1)], axis=0
    )
    summed = jnp.concatenate([dot_t(left, own_ref[...]), dot_t(left, other_ref[...])], axis=1)
    row, col = iota((2 * COLS, 2 * COLS), 0), iota((2 * COLS, 2 * COLS), 1)
    dest = row // (2 * CUT)
    within = row - dest * (2 * CUT)
    source = dest * CUT + jnp.where(within >= CUT, within - CUT + COLS, within)
    order = jnp.where(col == source, 1.0, 0.0).astype(BF)
    out_ref[...] = dot(order, summed.astype(BF)).astype(BF)


def operator_body(mix_ref, dop_ref, beam_ref, high_ref, low_ref):
    real, imag = [], []
    for c in range(CHAN):
        mr, mi = mix_ref[0, c : c + 1, :], mix_ref[1, c : c + 1, :]
        real.append(mr * dop_ref[0] - mi * dop_ref[1])
        imag.append(mr * dop_ref[1] + mi * dop_ref[0])
    both = jnp.concatenate(real + imag, axis=0)
    top = both.astype(BF)
    rest = (both - top.astype(F32)).astype(BF)
    by_real = dot(top, beam_ref[0]) + dot(rest, beam_ref[0])
    by_imag = dot(top, beam_ref[1]) + dot(rest, beam_ref[1])
    whole = jnp.concatenate(
        [by_real[:256] - by_imag[256:], by_real[256:] + by_imag[:256]], axis=1
    )
    top = whole.astype(BF)
    high_ref[...] = top
    low_ref[...] = (whole - top.astype(F32)).astype(BF)


def band_body(offset_ref, weight_ref, out_ref):
    strip = 32
    offset = jnp.broadcast_to(offset_ref[0], (strip, ANG))
    for start in range(0, ANG, strip):
        step = iota((strip, ANG), 0) + start - offset
        hits = [step == j for j in range(BAND)]
        for c in range(2):
            for part in range(2):
                value = jnp.zeros((strip, ANG), F32)
                for j in range(BAND):
                    value = jnp.where(hits[j], weight_ref[0, c, part, j : j + 1, :], value)
                out_ref[
                    0, c * ANG + start : c * ANG + start + strip, part * ANG : (part + 1) * ANG
                ] = value.astype(BF)


def merge_body(me_ref, comp_ref, high_ref, low_ref, band_ref, out_ref, pulses):
    me = me_ref[0]
    row, col = iota((512, 2 * COLS), 0), iota((512, 2 * COLS), 1)
    j = row & 15
    source = (row >> 5) * (2 * CUT) + ((row >> 4) & 1) * CUT + j
    order = jnp.where((col == source) & (j < CUT), 1.0, 0.0).astype(BF)
    apart = dot(order, comp_ref[...])
    for x in range(2):
        for part in range(2):
            blocks = []
            for c in range(CHAN):
                at = ((x * 8 + c) * 2 + part) * PAD
                blocks.append(apart[at : at + PAD])
            for q in range(8):
                n = x * 8 + (((q & 3) * 2 + (q >> 2)) ^ me)
                pulses[part, n] = jnp.concatenate(
                    [b[:, q * 32 : (q + 1) * 32] for b in blocks], axis=1
                )
    pulse = pulses[...].reshape(2 * GROUP * PAD, 256).astype(BF)
    formed = dot(pulse, high_ref[...]) + dot(pulse, low_ref[...])
    half = GROUP * PAD
    real = formed[:half, :ANG] - formed[half:, ANG:]
    imag = formed[half:, :ANG] + formed[:half, ANG:]
    for level in range(LEVELS):
        inner = 1 << level
        outer = GROUP // (2 * inner)
        real = real.reshape(outer, 2, inner * PAD, ANG)
        imag = imag.reshape(outer, 2, inner * PAD, ANG)
        sides = [
            jnp.concatenate(
                [real[:, c].reshape(half // 2, ANG), imag[:, c].reshape(half // 2, ANG)], axis=0
            )
            for c in range(2)
        ]
        left = jnp.concatenate(sides, axis=1)
        top = left.astype(BF)
        rest = (left - top.astype(F32)).astype(BF)
        reals, imags = [], []
        for h in range(2):
            band = band_ref[2 * level + h]
            out = dot(top, band) + dot(rest, band)
            r = out[: half // 2, :ANG] - out[half // 2 :, ANG:]
            i = out[half // 2 :, :ANG] + out[: half // 2, ANG:]
            reals.append(r.reshape(outer, 1, inner * PAD, ANG))
            imags.append(i.reshape(outer, 1, inner * PAD, ANG))
        real = jnp.concatenate(reals, axis=1)
        imag = jnp.concatenate(imags, axis=1)
    real = real.reshape(GROUP, PAD, ANG)
    imag = imag.reshape(GROUP, PAD, ANG)
    power = real * real + imag * imag
    out_ref[...] = power[:, :CUT, :]


def despeckle_body(chan_ref, power_ref, rate_ref, out_ref, bins):
    for t in range(GROUP):
        bins[t * CUT : (t + 1) * CUT, :] = power_ref[t]
    current = bins[...]
    cell = iota((COLS, ANG), 0) + (chan_ref[0] * 128 - HALO)
    inside = (cell >= 0) & (cell < 1024)
    rate = jnp.broadcast_to(rate_ref[...], (COLS, ANG))
    for _ in range(PASSES):
        before = pltpu.roll(current, 1, 0)
        after = pltpu.roll(current, COLS - 1, 0)
        current = jnp.where(inside, current + rate * (before - 2.0 * current + after), 0.0)
    out_ref[...] = current[HALO : HALO + 128, :].T


def doppler_table():
    index = np.arange(PULSES)
    phase = np.float32(2.0 * np.pi / PULSES) * (
        index[:, None] * index[None, :] % PULSES
    ).astype(np.float32)
    factor = np.float32(1.0 / np.sqrt(PULSES))
    parts = np.stack([np.cos(phase) * factor, -np.sin(phase) * factor])
    return parts.astype(ml_dtypes.bfloat16).astype(np.float32)


def flipped(value, axis, mask):
    pairs = [(source, source ^ mask) for source in range(lax.axis_size(axis))]
    return lax.ppermute(value, axis, pairs)


def exchange(value, axes):
    return lax.all_to_all(value, axes, split_axis=0, concat_axis=0, tiled=True)


def local(
    raw_pulses, range_filter, channel_mix, steer_angles, band_offsets, band_weights, smoothing
):
    raw = pl.pallas_call(
        raw_body,
        out_shape=jax.ShapeDtypeStruct((PULSES, 4096), BF),
        in_specs=[WHOLE],
        out_specs=WHOLE,
        name="raw_order",
    )(raw_pulses.reshape(2, PULSES, 2048))
    own = jnp.concatenate([raw] + [flipped(raw, "y", mask) for mask in (1, 2, 3)], axis=0)
    other = flipped(own, "core", 1)

    rows = range_filter.reshape(8, 1024)
    rows = exchange(jnp.broadcast_to(rows[None], (16, 8, 1024)), ALONG_Z).reshape(128, 1024)
    picked = pl.pallas_call(
        pick_body,
        out_shape=jax.ShapeDtypeStruct((4, ROW, COLS, 128), BF),
        in_specs=[WHOLE],
        out_specs=WHOLE,
        compiler_params=params(24),
        name="pick_bins",
    )(rows)
    filters = exchange(picked.reshape(32, COLS, 128), PLANE)

    offset = jnp.arange(ANG, dtype=jnp.int32).astype(F32) - 0.5 * ANG
    phase = steer_angles[None, :] * offset[:, None]
    factor = 1.0 / np.sqrt(ANG)
    beams = jnp.stack([jnp.cos(phase) * factor, jnp.sin(phase) * factor]).astype(BF)
    mix = channel_mix.transpose(0, 3, 2, 1).reshape(2, CHAN, 256)
    doppler = jnp.asarray(np.tile(doppler_table().transpose(0, 2, 1), (1, 1, CHAN)))
    high, low = pl.pallas_call(
        operator_body,
        out_shape=[jax.ShapeDtypeStruct((256, 2 * ANG), BF)] * 2,
        in_specs=[WHOLE] * 3,
        out_specs=[WHOLE] * 2,
        name="operator",
    )(mix, doppler, beams)
    weights = band_weights.reshape(LEVELS, 2, 2, 2, ANG, BAND).transpose(0, 3, 1, 2, 5, 4)
    band = pl.pallas_call(
        band_body,
        grid=(2 * LEVELS,),
        out_shape=jax.ShapeDtypeStruct((2 * LEVELS, 2 * ANG, 2 * ANG), BF),
        in_specs=[
            pl.BlockSpec((1, 1, ANG), lambda i: (i, 0, 0)),
            pl.BlockSpec((1, 2, 2, BAND, ANG), lambda i: (i, 0, 0, 0, 0)),
        ],
        out_specs=pl.BlockSpec((1, 2 * ANG, 2 * ANG), lambda i: (i, 0, 0)),
        name="band",
    )(
        band_offsets.reshape(2 * LEVELS, 1, ANG),
        weights.reshape(2 * LEVELS, 2, 2, BAND, ANG),
    )

    compressed = pl.pallas_call(
        compress_body,
        out_shape=jax.ShapeDtypeStruct((2 * COLS, 256), BF),
        in_specs=[WHOLE] * 3,
        out_specs=WHOLE,
        compiler_params=params(40),
        name="compress",
    )(filters, own, other)
    compressed = exchange(compressed.reshape(16, 2 * CUT, 256), ("x0", "chan"))
    me = (lax.axis_index("y") * 2 + lax.axis_index("core")).astype(jnp.int32).reshape(1)
    power = pl.pallas_call(
        merge_body,
        out_shape=jax.ShapeDtypeStruct((GROUP, CUT, ANG), F32),
        in_specs=[SCALAR] + [WHOLE] * 4,
        out_specs=WHOLE,
        scratch_shapes=[pltpu.VMEM((2, GROUP, PAD, 256), F32)],
        compiler_params=params(40),
        name="merge",
    )(me, compressed.reshape(2 * COLS, 256), high, low, band)
    power = exchange(power, MERGE)
    chan = lax.axis_index("chan").astype(jnp.int32).reshape(1)
    return pl.pallas_call(
        despeckle_body,
        out_shape=jax.ShapeDtypeStruct((ANG, 128), F32),
        in_specs=[SCALAR] + [WHOLE] * 2,
        out_specs=WHOLE,
        scratch_shapes=[pltpu.VMEM((COLS, ANG), F32)],
        name="despeckle",
    )(chan, power, smoothing.reshape(1, ANG))


def solution(mesh):
    split = Mesh(mesh.devices.reshape(2, 2, 2, 4, 2, mesh.shape["chan"]), AXES)
    placed = (
        P(None, SUB, "chan", None),
        P(None, AXES, None),
        P(),
        P(),
        P(),
        P(),
        P(SUB),
    )
    return jax.shard_map(
        local, mesh=split, in_specs=placed, out_specs=P(SUB, "chan"), check_vma=False
    )
```

```python
import functools

import jax
import jax.numpy as jnp
import ml_dtypes
import numpy as np
from jax import lax
from jax.experimental import pallas as pl
from jax.experimental.pallas import tpu as pltpu
from jax.sharding import Mesh
from jax.sharding import PartitionSpec as P

ANG = 256
BAND = 8
LEVELS = 4
PASSES = 3
PULSES = 32
CHAN = 8
GROUP = 16
ROW = 8
CUT = 9
PAD = 16
HALO = 8
COLS = GROUP * CUT
AXES = ("zh", "x1", "x0", "y", "core", "chan")
SUB = ("zh", "x1", "x0", "y", "core")
ALONG_Z = ("zh", "chan")
PLANE = ("x1", "x0", "y", "core")
MERGE = ("x0", "y", "core")
BF = jnp.bfloat16
F32 = jnp.float32
WHOLE = pl.BlockSpec(memory_space=pltpu.VMEM)
LEFT = pl.BlockSpec(memory_space=pltpu.HBM)
SCALAR = pl.BlockSpec(memory_space=pltpu.SMEM)


def params(mib):
    return pltpu.CompilerParams(vmem_limit_bytes=mib << 20)


def iota(shape, dim):
    return lax.broadcasted_iota(jnp.int32, shape, dim)


def dot(left, right):
    return jnp.dot(left, right, preferred_element_type=F32)


def dot_t(left, right):
    return lax.dot_general(left, right, (((1,), (1,)), ((), ())), preferred_element_type=F32)


def raw_body(raw_ref, out_ref):
    row, col = iota((512, 512), 0), iota((512, 512), 1)
    quarter, part, half, k = col >> 7, (col >> 6) & 1, (col >> 5) & 1, col & 31
    source = part * 256 + half * 128 + quarter * 32 + k
    sign = jnp.where(part == 1, -1.0, 1.0)
    order = jnp.where(row == source, sign, 0.0).astype(BF)
    rows = []
    for u in range(8):
        rows.append(
            jnp.concatenate(
                [
                    raw_ref[part, :, half * 1024 + u * 128 : half * 1024 + (u + 1) * 128]
                    for part in range(2)
                    for half in range(2)
                ],
                axis=1,
            )
        )
    moved = dot(jnp.concatenate(rows, axis=0), order).astype(BF)
    for u in range(8):
        out_ref[:, u * 512 : (u + 1) * 512] = moved[u * 32 : (u + 1) * 32]


def copies_body(filter_ref, out_ref):
    rows = filter_ref[...].astype(F32)
    rows = jnp.concatenate([rows[0], rows[1]], axis=0).astype(BF)
    for z in range(16):
        out_ref[z] = rows


def pick_body(filter_ref, out_ref):
    i, k = iota((128, 128), 0), iota((128, 128), 1)
    source = (((i >> 5) & 1) * 8 + ((i >> 2) & 7)) * 8 + (i >> 6) * 4 + (i & 3)
    rows = dot(jnp.where(k == source, 1.0, 0.0).astype(BF), filter_ref[...]).astype(BF)
    bins = iota((COLS, 1024), 1)
    r = iota((COLS, 1024), 0)
    dest = r // CUT
    first = 128 * (dest & 7) - HALO + 8 * CUT * (dest >> 3) + r - dest * CUT
    for g in range(ROW):
        pick = jnp.where(bins == first + CUT * g, 1.0, 0.0).astype(BF)
        block = dot_t(pick, rows).astype(BF)
        for x in range(4):
            out_ref[x, g] = block


def compress_body(filter_ref, own_ref, other_ref, out_ref):
    first, second = [], []
    for s in range(32):
        block = filter_ref[s]
        first.append(block)
        second.append(jnp.concatenate([block[:, 64:], -block[:, :64]], axis=1))
    left = jnp.concatenate(
        [jnp.concatenate(first, axis=1), jnp.concatenate(second, axis=1)], axis=0
    )
    summed = jnp.concatenate([dot_t(left, own_ref[...]), dot_t(left, other_ref[...])], axis=1)
    row, col = iota((32 * GROUP, 2 * COLS), 0), iota((32 * GROUP, 2 * COLS), 1)
    within = row & 31
    source = (row >> 5) * CUT + jnp.where(within >= CUT, within - CUT + COLS, within)
    order = jnp.where(col == source, 1.0, 0.0).astype(BF)
    moved = dot(order, summed.astype(BF)).astype(BF)
    for dest in range(GROUP):
        out_ref[dest] = moved[dest * 32 : dest * 32 + 2 * CUT]


def operator_body(mix_ref, dop_ref, beam_ref, out_ref):
    real, imag = [], []
    for c in range(CHAN):
        mr, mi = mix_ref[0, c : c + 1, :], mix_ref[1, c : c + 1, :]
        real.append(mr * dop_ref[0] - mi * dop_ref[1])
        imag.append(mr * dop_ref[1] + mi * dop_ref[0])
    both = jnp.concatenate(real + imag, axis=0)
    top = both.astype(BF)
    rest = (both - top.astype(F32)).astype(BF)
    by_real = dot(top, beam_ref[0]) + dot(rest, beam_ref[0])
    by_imag = dot(top, beam_ref[1]) + dot(rest, beam_ref[1])
    whole = jnp.concatenate(
        [by_real[:256] - by_imag[256:], by_real[256:] + by_imag[:256]], axis=1
    )
    top = whole.astype(BF)
    out_ref[0] = top
    out_ref[1] = (whole - top.astype(F32)).astype(BF)


def band_body(offset_ref, weight_ref, out_ref):
    strip = 32
    offset = jnp.broadcast_to(offset_ref[0], (strip, ANG))
    for start in range(0, ANG, strip):
        step = iota((strip, ANG), 0) + start - offset
        hits = [step == j for j in range(BAND)]
        for c in range(2):
            for part in range(2):
                value = jnp.zeros((strip, ANG), F32)
                for j in range(BAND):
                    value = jnp.where(hits[j], weight_ref[0, c, part, j : j + 1, :], value)
                out_ref[
                    0, c * ANG + start : c * ANG + start + strip, part * ANG : (part + 1) * ANG
                ] = value.astype(BF)


def merge_body(me_ref, comp_ref, operator_far, band_far, out_ref, pulses, operator, band, sems):
    copies = [pltpu.make_async_copy(operator_far, operator, sems.at[0])]
    for level in range(LEVELS):
        span = slice(2 * level, 2 * level + 2)
        copies.append(
            pltpu.make_async_copy(band_far.at[span], band.at[span], sems.at[1 + level])
        )
    for copy in copies:
        copy.start()
    me = me_ref[0]
    row, col = iota((512, 2 * COLS), 0), iota((512, 2 * COLS), 1)
    j = row & 15
    source = (row >> 5) * (2 * CUT) + ((row >> 4) & 1) * CUT + j
    order = jnp.where((col == source) & (j < CUT), 1.0, 0.0).astype(BF)
    apart = dot(order, comp_ref[...])
    for x in range(2):
        for part in range(2):
            blocks = []
            for c in range(CHAN):
                at = ((x * 8 + c) * 2 + part) * PAD
                blocks.append(apart[at : at + PAD])
            for q in range(8):
                n = x * 8 + (((q & 3) * 2 + (q >> 2)) ^ me)
                pulses[part, n] = jnp.concatenate(
                    [b[:, q * 32 : (q + 1) * 32] for b in blocks], axis=1
                )
    pulse = pulses[...].reshape(2 * GROUP * PAD, 256).astype(BF)
    copies[0].wait()
    formed = dot(pulse, operator[0]) + dot(pulse, operator[1])
    half = GROUP * PAD
    real = formed[:half, :ANG] - formed[half:, ANG:]
    imag = formed[half:, :ANG] + formed[:half, ANG:]
    for level in range(LEVELS):
        inner = 1 << level
        outer = GROUP // (2 * inner)
        real = real.reshape(outer, 2, inner * PAD, ANG)
        imag = imag.reshape(outer, 2, inner * PAD, ANG)
        sides = [
            jnp.concatenate(
                [real[:, c].reshape(half // 2, ANG), imag[:, c].reshape(half // 2, ANG)], axis=0
            )
            for c in range(2)
        ]
        left = jnp.concatenate(sides, axis=1)
        top = left.astype(BF)
        rest = (left - top.astype(F32)).astype(BF)
        reals, imags = [], []
        copies[1 + level].wait()
        for h in range(2):
            weight = band[2 * level + h]
            out = dot(top, weight) + dot(rest, weight)
            r = out[: half // 2, :ANG] - out[half // 2 :, ANG:]
            i = out[half // 2 :, :ANG] + out[: half // 2, ANG:]
            reals.append(r.reshape(outer, 1, inner * PAD, ANG))
            imags.append(i.reshape(outer, 1, inner * PAD, ANG))
        real = jnp.concatenate(reals, axis=1)
        imag = jnp.concatenate(imags, axis=1)
    real = real.reshape(GROUP, PAD, ANG)
    imag = imag.reshape(GROUP, PAD, ANG)
    power = real * real + imag * imag
    out_ref[...] = power[:, :CUT, :]


def despeckle_body(chan_ref, power_ref, rate_ref, out_ref, bins):
    for t in range(GROUP):
        bins[t * CUT : (t + 1) * CUT, :] = power_ref[t]
    current = bins[...]
    cell = iota((COLS, ANG), 0) + (chan_ref[0] * 128 - HALO)
    inside = (cell >= 0) & (cell < 1024)
    rate = jnp.broadcast_to(rate_ref[...], (COLS, ANG))
    for _ in range(PASSES):
        before = pltpu.roll(current, 1, 0)
        after = pltpu.roll(current, COLS - 1, 0)
        current = jnp.where(inside, current + rate * (before - 2.0 * current + after), 0.0)
    out_ref[...] = current[HALO : HALO + 128, :].T


def doppler_table():
    index = np.arange(PULSES)
    phase = np.float32(2.0 * np.pi / PULSES) * (
        index[:, None] * index[None, :] % PULSES
    ).astype(np.float32)
    factor = np.float32(1.0 / np.sqrt(PULSES))
    parts = np.stack([np.cos(phase) * factor, -np.sin(phase) * factor])
    return parts.astype(ml_dtypes.bfloat16).astype(np.float32)


def flipped(value, axis, mask):
    pairs = [(source, source ^ mask) for source in range(lax.axis_size(axis))]
    return lax.ppermute(value, axis, pairs)


def exchange(value, axes):
    return lax.all_to_all(value, axes, split_axis=0, concat_axis=0, tiled=True)


def local(
    raw_pulses, range_filter, channel_mix, steer_angles, band_offsets, band_weights, smoothing
):
    raw = pl.pallas_call(
        raw_body,
        out_shape=jax.ShapeDtypeStruct((PULSES, 4096), BF),
        in_specs=[WHOLE],
        out_specs=WHOLE,
        compiler_params=params(8),
        name="raw_order",
    )(raw_pulses.reshape(2, PULSES, 2048))
    own = jnp.concatenate([raw] + [flipped(raw, "y", mask) for mask in (1, 2, 3)], axis=0)
    other = flipped(own, "core", 1)

    rows = pl.pallas_call(
        copies_body,
        out_shape=jax.ShapeDtypeStruct((16, 8, 1024), BF),
        in_specs=[WHOLE],
        out_specs=WHOLE,
        compiler_params=params(2),
        name="copies",
    )(range_filter)
    rows = exchange(rows, ALONG_Z).reshape(128, 1024)
    picked = pl.pallas_call(
        pick_body,
        out_shape=jax.ShapeDtypeStruct((4, ROW, COLS, 128), BF),
        in_specs=[WHOLE],
        out_specs=WHOLE,
        compiler_params=params(8),
        name="pick_bins",
    )(rows)
    filters = exchange(picked.reshape(32, COLS, 128), PLANE)

    offset = jnp.arange(ANG, dtype=jnp.int32).astype(F32) - 0.5 * ANG
    phase = steer_angles[None, :] * offset[:, None]
    factor = 1.0 / np.sqrt(ANG)
    beams = jnp.stack([jnp.cos(phase) * factor, jnp.sin(phase) * factor]).astype(BF)
    mix = channel_mix.transpose(0, 3, 2, 1).reshape(2, CHAN, 256)
    doppler = jnp.asarray(np.tile(doppler_table().transpose(0, 2, 1), (1, 1, CHAN)))
    operator = pl.pallas_call(
        operator_body,
        out_shape=jax.ShapeDtypeStruct((2, 256, 2 * ANG), BF),
        in_specs=[WHOLE] * 3,
        out_specs=WHOLE,
        compiler_params=params(8),
        name="operator",
    )(mix, doppler, beams)
    weights = band_weights.reshape(LEVELS, 2, 2, 2, ANG, BAND).transpose(0, 3, 1, 2, 5, 4)
    band = pl.pallas_call(
        band_body,
        grid=(2 * LEVELS,),
        out_shape=jax.ShapeDtypeStruct((2 * LEVELS, 2 * ANG, 2 * ANG), BF),
        in_specs=[
            pl.BlockSpec((1, 1, ANG), lambda i: (i, 0, 0)),
            pl.BlockSpec((1, 2, 2, BAND, ANG), lambda i: (i, 0, 0, 0, 0)),
        ],
        out_specs=pl.BlockSpec((1, 2 * ANG, 2 * ANG), lambda i: (i, 0, 0)),
        compiler_params=params(4),
        name="band",
    )(
        band_offsets.reshape(2 * LEVELS, 1, ANG),
        weights.reshape(2 * LEVELS, 2, 2, BAND, ANG),
    )

    filters, operator, band = lax.optimization_barrier((filters, operator, band))
    compressed = pl.pallas_call(
        compress_body,
        out_shape=jax.ShapeDtypeStruct((GROUP, 2 * CUT, 256), BF),
        in_specs=[WHOLE] * 3,
        out_specs=WHOLE,
        compiler_params=params(16),
        name="compress",
    )(filters, own, other)
    compressed = exchange(compressed, ("x0", "chan"))
    me = (lax.axis_index("y") * 2 + lax.axis_index("core")).astype(jnp.int32).reshape(1)
    power = pl.pallas_call(
        merge_body,
        out_shape=jax.ShapeDtypeStruct((GROUP, CUT, ANG), F32),
        in_specs=[SCALAR, WHOLE, LEFT, LEFT],
        out_specs=WHOLE,
        scratch_shapes=[
            pltpu.VMEM((2, GROUP, PAD, 256), F32),
            pltpu.VMEM((2, 256, 2 * ANG), BF),
            pltpu.VMEM((2 * LEVELS, 2 * ANG, 2 * ANG), BF),
            pltpu.SemaphoreType.DMA((1 + LEVELS,)),
        ],
        compiler_params=params(58),
        name="merge",
    )(me, compressed.reshape(2 * COLS, 256), operator, band)
    power = exchange(power, MERGE)
    chan = lax.axis_index("chan").astype(jnp.int32).reshape(1)
    return pl.pallas_call(
        despeckle_body,
        out_shape=jax.ShapeDtypeStruct((ANG, 128), F32),
        in_specs=[SCALAR] + [WHOLE] * 2,
        out_specs=WHOLE,
        scratch_shapes=[pltpu.VMEM((COLS, ANG), F32)],
        compiler_params=params(4),
        name="despeckle",
    )(chan, power, smoothing.reshape(1, ANG))


def solution(mesh):
    split = Mesh(mesh.devices.reshape(2, 2, 2, 4, 2, mesh.shape["chan"]), AXES)
    placed = (
        P(None, SUB, "chan", None),
        P(None, AXES, None),
        P(),
        P(),
        P(),
        P(),
        P(SUB),
    )
    return jax.shard_map(
        local, mesh=split, in_specs=placed, out_specs=P(SUB, "chan"), check_vma=False
    )
```

```python
import functools

import jax
import jax.numpy as jnp
import ml_dtypes
import numpy as np
from jax import lax
from jax.experimental import pallas as pl
from jax.experimental.pallas import tpu as pltpu
from jax.sharding import Mesh
from jax.sharding import PartitionSpec as P

ANG = 256
BAND = 8
LEVELS = 4
PASSES = 3
PULSES = 32
CHAN = 8
GROUP = 16
ROW = 8
CUT = 9
PAD = 16
SENT = 24
HALO = 8
COLS = GROUP * CUT
REVERSED = [8 * (m & 1) + 4 * (m >> 1 & 1) + 2 * (m >> 2 & 1) + (m >> 3) for m in range(GROUP)]
AXES = ("zh", "x1", "x0", "y", "core", "chan")
SUB = ("zh", "x1", "x0", "y", "core")
ALONG_Z = ("zh", "chan")
PLANE = ("x1", "x0", "y", "core")
MERGE = ("x0", "y", "core")
BF = jnp.bfloat16
F32 = jnp.float32
WHOLE = pl.BlockSpec(memory_space=pltpu.VMEM)
LEFT = pl.BlockSpec(memory_space=pltpu.HBM)
SCALAR = pl.BlockSpec(memory_space=pltpu.SMEM)


def params(mib):
    return pltpu.CompilerParams(vmem_limit_bytes=mib << 20)


def iota(shape, dim):
    return lax.broadcasted_iota(jnp.int32, shape, dim)


def dot(left, right):
    return jnp.dot(left, right, preferred_element_type=F32)


def dot_t(left, right):
    return lax.dot_general(left, right, (((1,), (1,)), ((), ())), preferred_element_type=F32)


def raw_body(raw_ref, out_ref):
    row, col = iota((512, 512), 0), iota((512, 512), 1)
    quarter, part, half, k = col >> 7, (col >> 6) & 1, (col >> 5) & 1, col & 31
    source = part * 256 + half * 128 + quarter * 32 + k
    sign = jnp.where(part == 1, -1.0, 1.0)
    order = jnp.where(row == source, sign, 0.0).astype(BF)
    rows = []
    for u in range(8):
        rows.append(
            jnp.concatenate(
                [
                    raw_ref[part, :, half * 1024 + u * 128 : half * 1024 + (u + 1) * 128]
                    for part in range(2)
                    for half in range(2)
                ],
                axis=1,
            )
        )
    moved = dot(jnp.concatenate(rows, axis=0), order).astype(BF)
    for u in range(8):
        out_ref[:, u * 512 : (u + 1) * 512] = moved[u * 32 : (u + 1) * 32]


def copies_body(filter_ref, out_ref):
    rows = filter_ref[...].astype(F32)
    rows = jnp.concatenate([rows[0], rows[1]], axis=0).astype(BF)
    for z in range(16):
        out_ref[z] = rows


def pick_body(filter_ref, out_ref):
    i, k = iota((128, 128), 0), iota((128, 128), 1)
    source = (((i >> 5) & 1) * 8 + ((i >> 2) & 7)) * 8 + (i >> 6) * 4 + (i & 3)
    rows = dot(jnp.where(k == source, 1.0, 0.0).astype(BF), filter_ref[...]).astype(BF)
    bins = iota((COLS, 1024), 1)
    r = iota((COLS, 1024), 0)
    dest = r // CUT
    first = 128 * (dest & 7) - HALO + 8 * CUT * (dest >> 3) + r - dest * CUT
    for g in range(ROW):
        pick = jnp.where(bins == first + CUT * g, 1.0, 0.0).astype(BF)
        block = dot_t(pick, rows).astype(BF)
        for x in range(4):
            out_ref[x, g] = block


def compress_body(filter_ref, own_ref, other_ref, out_ref, pulses):
    pulses[:128, :] = own_ref[...]
    pulses[128:, :] = other_ref[...]
    first, second = [], []
    for s in range(32):
        block = filter_ref[s]
        first.append(block)
        second.append(jnp.concatenate([block[:, 64:], -block[:, :64]], axis=1))
    left = jnp.concatenate(
        [jnp.concatenate(first, axis=1), jnp.concatenate(second, axis=1)], axis=0
    )
    summed = dot_t(left, pulses[...])
    row, col = iota((32 * GROUP, 2 * COLS), 0), iota((32 * GROUP, 2 * COLS), 1)
    within = row & 31
    source = (row >> 5) * CUT + jnp.where(within >= CUT, within - CUT + COLS, within)
    order = jnp.where((col == source) & (within < 2 * CUT), 1.0, 0.0).astype(BF)
    moved = dot(order, summed.astype(BF)).astype(BF)
    for dest in range(GROUP):
        out_ref[dest] = moved[dest * 32 : dest * 32 + SENT]


def operator_body(mix_ref, dop_ref, beam_ref, out_ref):
    real, imag = [], []
    for c in range(CHAN):
        mr, mi = mix_ref[0, c : c + 1, :], mix_ref[1, c : c + 1, :]
        real.append(mr * dop_ref[0] - mi * dop_ref[1])
        imag.append(mr * dop_ref[1] + mi * dop_ref[0])
    both = jnp.concatenate(real + imag, axis=0)
    top = both.astype(BF)
    rest = (both - top.astype(F32)).astype(BF)
    by_real = dot(top, beam_ref[0]) + dot(rest, beam_ref[0])
    by_imag = dot(top, beam_ref[1]) + dot(rest, beam_ref[1])
    whole = jnp.concatenate(
        [by_real[:256] - by_imag[256:], by_real[256:] + by_imag[:256]], axis=1
    )
    top = whole.astype(BF)
    out_ref[0] = top
    out_ref[1] = (whole - top.astype(F32)).astype(BF)


def band_body(offset_ref, weight_ref, out_ref):
    strip = 32
    offset = jnp.broadcast_to(offset_ref[0], (strip, ANG))
    for start in range(0, ANG, strip):
        step = iota((strip, ANG), 0) + start - offset
        hits = [step == j for j in range(BAND)]
        for c in range(2):
            for part in range(2):
                value = jnp.zeros((strip, ANG), F32)
                for j in range(BAND):
                    value = jnp.where(hits[j], weight_ref[0, c, part, j : j + 1, :], value)
                out_ref[
                    0, c * ANG + start : c * ANG + start + strip, part * ANG : (part + 1) * ANG
                ] = value.astype(BF)


def merge_body(me_ref, comp_ref, operator_ref, band_far, out_ref, pulses, band, sems):
    copies = []
    for level in range(LEVELS):
        span = slice(2 * level, 2 * level + 2)
        copies.append(pltpu.make_async_copy(band_far.at[span], band.at[span], sems.at[level]))
    for copy in copies:
        copy.start()
    me = me_ref[0]
    row, col = iota((512, SENT * GROUP), 0), iota((512, SENT * GROUP), 1)
    j = row & 15
    source = (row >> 5) * SENT + ((row >> 4) & 1) * CUT + j
    order = jnp.where((col == source) & (j < CUT), 1.0, 0.0).astype(BF)
    apart = dot(order, comp_ref[...])
    for x in range(2):
        for part in range(2):
            blocks = []
            for c in range(CHAN):
                at = ((x * 8 + c) * 2 + part) * PAD
                blocks.append(apart[at : at + PAD])
            for q in range(8):
                n = x * 8 + (((q & 3) * 2 + (q >> 2)) ^ me)
                pulses[part, n] = jnp.concatenate(
                    [b[:, q * 32 : (q + 1) * 32] for b in blocks], axis=1
                )
    pulse = pulses[...].reshape(2 * GROUP * PAD, 256).astype(BF)
    formed = dot(pulse, operator_ref[0]) + dot(pulse, operator_ref[1])
    half = GROUP * PAD
    real = formed[:half, :ANG] - formed[half:, ANG:]
    imag = formed[half:, :ANG] + formed[:half, ANG:]
    real, imag = [
        jnp.concatenate([part[n * PAD : n * PAD + CUT] for n in REVERSED], axis=0)
        for part in (real, imag)
    ]
    half = COLS // 2
    for level in range(LEVELS):
        block = COLS >> level
        sides = []
        for c in range(2):
            starts = [k * block + c * (block // 2) for k in range(1 << level)]
            sides.append(
                jnp.concatenate(
                    [part[at : at + block // 2] for part in (real, imag) for at in starts], axis=0
                )
            )
        left = jnp.concatenate(sides, axis=1)
        top = left.astype(BF)
        rest = (left - top.astype(F32)).astype(BF)
        reals, imags = [], []
        copies[level].wait()
        for h in range(2):
            weight = band[2 * level + h]
            out = dot(top, weight) + dot(rest, weight)
            reals.append(out[:half, :ANG] - out[half:, ANG:])
            imags.append(out[half:, :ANG] + out[:half, ANG:])
        real = jnp.concatenate(reals, axis=0)
        imag = jnp.concatenate(imags, axis=0)
    power = real * real + imag * imag
    rest = jnp.zeros((PAD - CUT, ANG), F32)
    for n in range(GROUP):
        out_ref[n] = jnp.concatenate([power[n * CUT : (n + 1) * CUT], rest], axis=0).astype(BF)


def despeckle_body(chan_ref, power_ref, rate_ref, out_ref, bins):
    for t in range(GROUP):
        bins[t * CUT : (t + 1) * CUT, :] = power_ref[t].astype(F32)[:CUT]
    current = bins[...]
    cell = iota((COLS, ANG), 0) + (chan_ref[0] * 128 - HALO)
    inside = (cell >= 0) & (cell < 1024)
    rate = jnp.broadcast_to(rate_ref[...], (COLS, ANG))
    for _ in range(PASSES):
        before = pltpu.roll(current, 1, 0)
        after = pltpu.roll(current, COLS - 1, 0)
        current = jnp.where(inside, current + rate * (before - 2.0 * current + after), 0.0)
    out_ref[...] = current[HALO : HALO + 128, :].T


def doppler_table():
    index = np.arange(PULSES)
    phase = np.float32(2.0 * np.pi / PULSES) * (
        index[:, None] * index[None, :] % PULSES
    ).astype(np.float32)
    factor = np.float32(1.0 / np.sqrt(PULSES))
    parts = np.stack([np.cos(phase) * factor, -np.sin(phase) * factor])
    return parts.astype(ml_dtypes.bfloat16).astype(np.float32)


def flipped(value, axis, mask):
    pairs = [(source, source ^ mask) for source in range(lax.axis_size(axis))]
    return lax.ppermute(value, axis, pairs)


def exchange(value, axes):
    return lax.all_to_all(value, axes, split_axis=0, concat_axis=0, tiled=True)


def local(
    raw_pulses, range_filter, channel_mix, steer_angles, band_offsets, band_weights, smoothing
):
    raw = pl.pallas_call(
        raw_body,
        out_shape=jax.ShapeDtypeStruct((PULSES, 4096), BF),
        in_specs=[WHOLE],
        out_specs=WHOLE,
        compiler_params=params(8),
        name="raw_order",
    )(raw_pulses.reshape(2, PULSES, 2048))
    own = jnp.concatenate([raw] + [flipped(raw, "y", mask) for mask in (1, 2, 3)], axis=0)
    other = flipped(own, "core", 1)

    rows = pl.pallas_call(
        copies_body,
        out_shape=jax.ShapeDtypeStruct((16, 8, 1024), BF),
        in_specs=[WHOLE],
        out_specs=WHOLE,
        compiler_params=params(2),
        name="copies",
    )(range_filter)
    rows = exchange(rows, ALONG_Z).reshape(128, 1024)
    picked = pl.pallas_call(
        pick_body,
        out_shape=jax.ShapeDtypeStruct((4, ROW, COLS, 128), BF),
        in_specs=[WHOLE],
        out_specs=WHOLE,
        compiler_params=params(8),
        name="pick_bins",
    )(rows)
    filters = exchange(picked.reshape(32, COLS, 128), PLANE)

    offset = jnp.arange(ANG, dtype=jnp.int32).astype(F32) - 0.5 * ANG
    phase = steer_angles[None, :] * offset[:, None]
    factor = 1.0 / np.sqrt(ANG)
    beams = jnp.stack([jnp.cos(phase) * factor, jnp.sin(phase) * factor]).astype(BF)
    mix = channel_mix.transpose(0, 3, 2, 1).reshape(2, CHAN, 256)
    doppler = jnp.asarray(np.tile(doppler_table().transpose(0, 2, 1), (1, 1, CHAN)))
    operator = pl.pallas_call(
        operator_body,
        out_shape=jax.ShapeDtypeStruct((2, 256, 2 * ANG), BF),
        in_specs=[WHOLE] * 3,
        out_specs=WHOLE,
        compiler_params=params(8),
        name="operator",
    )(mix, doppler, beams)
    weights = band_weights.reshape(LEVELS, 2, 2, 2, ANG, BAND).transpose(0, 3, 1, 2, 5, 4)
    band = pl.pallas_call(
        band_body,
        grid=(2 * LEVELS,),
        out_shape=jax.ShapeDtypeStruct((2 * LEVELS, 2 * ANG, 2 * ANG), BF),
        in_specs=[
            pl.BlockSpec((1, 1, ANG), lambda i: (i, 0, 0)),
            pl.BlockSpec((1, 2, 2, BAND, ANG), lambda i: (i, 0, 0, 0, 0)),
        ],
        out_specs=pl.BlockSpec((1, 2 * ANG, 2 * ANG), lambda i: (i, 0, 0)),
        compiler_params=params(4),
        name="band",
    )(
        band_offsets.reshape(2 * LEVELS, 1, ANG),
        weights.reshape(2 * LEVELS, 2, 2, BAND, ANG),
    )

    filters, operator, band = lax.optimization_barrier((filters, operator, band))
    compressed = pl.pallas_call(
        compress_body,
        out_shape=jax.ShapeDtypeStruct((GROUP, SENT, 256), BF),
        in_specs=[WHOLE] * 3,
        out_specs=WHOLE,
        scratch_shapes=[pltpu.VMEM((256, 4096), BF)],
        compiler_params=params(16),
        name="compress",
    )(filters, own, other)
    compressed = exchange(compressed, ("x0", "chan"))
    me = (lax.axis_index("y") * 2 + lax.axis_index("core")).astype(jnp.int32).reshape(1)
    power = pl.pallas_call(
        merge_body,
        out_shape=jax.ShapeDtypeStruct((GROUP, PAD, ANG), BF),
        in_specs=[SCALAR, WHOLE, WHOLE, LEFT],
        out_specs=WHOLE,
        scratch_shapes=[
            pltpu.VMEM((2, GROUP, PAD, 256), F32),
            pltpu.VMEM((2 * LEVELS, 2 * ANG, 2 * ANG), BF),
            pltpu.SemaphoreType.DMA((LEVELS,)),
        ],
        compiler_params=params(52),
        name="merge",
    )(me, compressed.reshape(GROUP * SENT, 256), operator, band)
    power = exchange(power, MERGE)
    chan = lax.axis_index("chan").astype(jnp.int32).reshape(1)
    return pl.pallas_call(
        despeckle_body,
        out_shape=jax.ShapeDtypeStruct((ANG, 128), F32),
        in_specs=[SCALAR] + [WHOLE] * 2,
        out_specs=WHOLE,
        scratch_shapes=[pltpu.VMEM((COLS, ANG), F32)],
        compiler_params=params(4),
        name="despeckle",
    )(chan, power, smoothing.reshape(1, ANG))


def solution(mesh):
    split = Mesh(mesh.devices.reshape(2, 2, 2, 4, 2, mesh.shape["chan"]), AXES)
    placed = (
        P(None, SUB, "chan", None),
        P(None, AXES, None),
        P(),
        P(),
        P(),
        P(),
        P(SUB),
    )
    return jax.shard_map(
        local, mesh=split, in_specs=placed, out_specs=P(SUB, "chan"), check_vma=False
    )
```

```python
import functools

import jax
import jax.numpy as jnp
import ml_dtypes
import numpy as np
from jax import lax
from jax.experimental import pallas as pl
from jax.experimental.pallas import tpu as pltpu
from jax.sharding import Mesh
from jax.sharding import PartitionSpec as P

ANG = 256
BAND = 8
LEVELS = 4
PASSES = 3
PULSES = 32
CHAN = 8
GROUP = 16
ROW = 8
CUT = 9
PAD = 16
SENT = 24
HALO = 8
COLS = GROUP * CUT
REVERSED = [8 * (m & 1) + 4 * (m >> 1 & 1) + 2 * (m >> 2 & 1) + (m >> 3) for m in range(GROUP)]
AXES = ("zh", "x1", "x0", "y", "core", "chan")
SUB = ("zh", "x1", "x0", "y", "core")
ALONG_Z = ("zh", "chan")
PLANE = ("x1", "x0", "y", "core")
MERGE = ("x0", "y", "core")
BF = jnp.bfloat16
F32 = jnp.float32
WHOLE = pl.BlockSpec(memory_space=pltpu.VMEM)
LEFT = pl.BlockSpec(memory_space=pltpu.HBM)
SCALAR = pl.BlockSpec(memory_space=pltpu.SMEM)


def params(mib):
    return pltpu.CompilerParams(vmem_limit_bytes=mib << 20)


def iota(shape, dim):
    return lax.broadcasted_iota(jnp.int32, shape, dim)


def dot(left, right):
    return jnp.dot(left, right, preferred_element_type=F32)


def dot_t(left, right):
    return lax.dot_general(left, right, (((1,), (1,)), ((), ())), preferred_element_type=F32)


def raw_body(raw_ref, out_ref):
    row, col = iota((512, 512), 0), iota((512, 512), 1)
    quarter, part, half, k = col >> 7, (col >> 6) & 1, (col >> 5) & 1, col & 31
    source = part * 256 + half * 128 + quarter * 32 + k
    sign = jnp.where(part == 1, -1.0, 1.0)
    order = jnp.where(row == source, sign, 0.0).astype(BF)
    rows = []
    for u in range(8):
        rows.append(
            jnp.concatenate(
                [
                    raw_ref[part, :, half * 1024 + u * 128 : half * 1024 + (u + 1) * 128]
                    for part in range(2)
                    for half in range(2)
                ],
                axis=1,
            )
        )
    moved = dot(jnp.concatenate(rows, axis=0), order).astype(BF)
    for u in range(8):
        out_ref[:, u * 512 : (u + 1) * 512] = moved[u * 32 : (u + 1) * 32]


def copies_body(filter_far, out_far, sems):
    copies = [pltpu.make_async_copy(filter_far, out_far.at[z], sems.at[z]) for z in range(16)]
    for copy in copies:
        copy.start()
    for copy in copies:
        copy.wait()


def pick_body(filter_ref, out_far, ordered, picked, sems):
    for z in range(16):
        for part in range(2):
            at = part * 64 + z * 4
            ordered[at : at + 4, :] = filter_ref[z, part].astype(F32)
    rows = ordered[...].astype(BF)
    bins = iota((COLS, 1024), 1)
    r = iota((COLS, 1024), 0)
    dest = r // CUT
    first = 128 * (dest & 7) - HALO + 8 * CUT * (dest >> 3) + r - dest * CUT
    copies = []
    for g in range(ROW):
        pick = jnp.where(bins == first + CUT * g, 1.0, 0.0).astype(BF)
        picked[g] = dot_t(pick, rows).astype(BF)
        for x in range(4):
            copy = pltpu.make_async_copy(picked.at[g], out_far.at[x, g], sems.at[x, g])
            copy.start()
            copies.append(copy)
    for copy in copies:
        copy.wait()


def compress_body(filter_ref, own_ref, other_ref, out_ref):
    first, second = [], []
    for s in range(32):
        block = filter_ref[s]
        first.append(block)
        second.append(jnp.concatenate([block[:, 64:], -block[:, :64]], axis=1))
    left = jnp.concatenate(
        [jnp.concatenate(first, axis=1), jnp.concatenate(second, axis=1)], axis=0
    )
    summed = jnp.concatenate([dot_t(left, own_ref[...]), dot_t(left, other_ref[...])], axis=1)
    row, col = iota((32 * GROUP, 2 * COLS), 0), iota((32 * GROUP, 2 * COLS), 1)
    within = row & 31
    source = (row >> 5) * CUT + jnp.where(within >= CUT, within - CUT + COLS, within)
    order = jnp.where((col == source) & (within < 2 * CUT), 1.0, 0.0).astype(BF)
    moved = dot(order, summed.astype(BF)).astype(BF)
    for dest in range(GROUP):
        out_ref[dest] = moved[dest * 32 : dest * 32 + SENT]


def operator_body(mix_ref, dop_ref, beam_ref, out_ref):
    real, imag = [], []
    for c in range(CHAN):
        mr, mi = mix_ref[0, c : c + 1, :], mix_ref[1, c : c + 1, :]
        real.append(mr * dop_ref[0] - mi * dop_ref[1])
        imag.append(mr * dop_ref[1] + mi * dop_ref[0])
    both = jnp.concatenate(real + imag, axis=0)
    top = both.astype(BF)
    rest = (both - top.astype(F32)).astype(BF)
    by_real = dot(top, beam_ref[0]) + dot(rest, beam_ref[0])
    by_imag = dot(top, beam_ref[1]) + dot(rest, beam_ref[1])
    whole = jnp.concatenate(
        [by_real[:256] - by_imag[256:], by_real[256:] + by_imag[:256]], axis=1
    )
    top = whole.astype(BF)
    out_ref[0] = top
    out_ref[1] = (whole - top.astype(F32)).astype(BF)


def band_body(offset_ref, weight_ref, out_ref):
    strip = 32
    offset = jnp.broadcast_to(offset_ref[0], (strip, ANG))
    for start in range(0, ANG, strip):
        step = iota((strip, ANG), 0) + start - offset
        hits = [step == j for j in range(BAND)]
        for c in range(2):
            for part in range(2):
                value = jnp.zeros((strip, ANG), F32)
                for j in range(BAND):
                    value = jnp.where(hits[j], weight_ref[0, c, part, j : j + 1, :], value)
                out_ref[
                    0, c * ANG + start : c * ANG + start + strip, part * ANG : (part + 1) * ANG
                ] = value.astype(BF)


def merge_body(me_ref, comp_ref, operator_ref, band_far, out_ref, pulses, band, sems):
    copies = []
    for level in range(LEVELS):
        span = slice(2 * level, 2 * level + 2)
        copies.append(pltpu.make_async_copy(band_far.at[span], band.at[span], sems.at[level]))
    for copy in copies:
        copy.start()
    me = me_ref[0]
    row, col = iota((512, SENT * GROUP), 0), iota((512, SENT * GROUP), 1)
    j = row & 15
    source = (row >> 5) * SENT + ((row >> 4) & 1) * CUT + j
    order = jnp.where((col == source) & (j < CUT), 1.0, 0.0).astype(BF)
    apart = dot(order, comp_ref[...])
    for x in range(2):
        for part in range(2):
            blocks = []
            for c in range(CHAN):
                at = ((x * 8 + c) * 2 + part) * PAD
                blocks.append(apart[at : at + PAD])
            for q in range(8):
                n = x * 8 + (((q & 3) * 2 + (q >> 2)) ^ me)
                pulses[part, n] = jnp.concatenate(
                    [b[:, q * 32 : (q + 1) * 32] for b in blocks], axis=1
                )
    pulse = pulses[...].reshape(2 * GROUP * PAD, 256).astype(BF)
    formed = dot(pulse, operator_ref[0]) + dot(pulse, operator_ref[1])
    half = GROUP * PAD
    real = formed[:half, :ANG] - formed[half:, ANG:]
    imag = formed[half:, :ANG] + formed[:half, ANG:]
    real, imag = [
        jnp.concatenate([part[n * PAD : n * PAD + CUT] for n in REVERSED], axis=0)
        for part in (real, imag)
    ]
    half = COLS // 2
    for level in range(LEVELS):
        block = COLS >> level
        sides = []
        for c in range(2):
            starts = [k * block + c * (block // 2) for k in range(1 << level)]
            sides.append(
                jnp.concatenate(
                    [part[at : at + block // 2] for part in (real, imag) for at in starts], axis=0
                )
            )
        left = jnp.concatenate(sides, axis=1)
        top = left.astype(BF)
        rest = (left - top.astype(F32)).astype(BF)
        reals, imags = [], []
        copies[level].wait()
        for h in range(2):
            weight = band[2 * level + h]
            out = dot(top, weight) + dot(rest, weight)
            reals.append(out[:half, :ANG] - out[half:, ANG:])
            imags.append(out[half:, :ANG] + out[:half, ANG:])
        real = jnp.concatenate(reals, axis=0)
        imag = jnp.concatenate(imags, axis=0)
    power = real * real + imag * imag
    rest = jnp.zeros((PAD - CUT, ANG), F32)
    for n in range(GROUP):
        out_ref[n] = jnp.concatenate([power[n * CUT : (n + 1) * CUT], rest], axis=0).astype(BF)


def despeckle_body(chan_ref, power_ref, rate_ref, out_ref, bins):
    for t in range(GROUP):
        bins[t * CUT : (t + 1) * CUT, :] = power_ref[t].astype(F32)[:CUT]
    current = bins[...]
    cell = iota((COLS, ANG), 0) + (chan_ref[0] * 128 - HALO)
    inside = (cell >= 0) & (cell < 1024)
    rate = jnp.broadcast_to(rate_ref[...], (COLS, ANG))
    for _ in range(PASSES):
        before = pltpu.roll(current, 1, 0)
        after = pltpu.roll(current, COLS - 1, 0)
        current = jnp.where(inside, current + rate * (before - 2.0 * current + after), 0.0)
    out_ref[...] = current[HALO : HALO + 128, :].T


def doppler_table():
    index = np.arange(PULSES)
    phase = np.float32(2.0 * np.pi / PULSES) * (
        index[:, None] * index[None, :] % PULSES
    ).astype(np.float32)
    factor = np.float32(1.0 / np.sqrt(PULSES))
    parts = np.stack([np.cos(phase) * factor, -np.sin(phase) * factor])
    return parts.astype(ml_dtypes.bfloat16).astype(np.float32)


def flipped(value, axis, mask):
    pairs = [(source, source ^ mask) for source in range(lax.axis_size(axis))]
    return lax.ppermute(value, axis, pairs)


def exchange(value, axes):
    return lax.all_to_all(value, axes, split_axis=0, concat_axis=0, tiled=True)


def local(
    raw_pulses, range_filter, channel_mix, steer_angles, band_offsets, band_weights, smoothing
):
    raw = pl.pallas_call(
        raw_body,
        out_shape=jax.ShapeDtypeStruct((PULSES, 4096), BF),
        in_specs=[WHOLE],
        out_specs=WHOLE,
        compiler_params=params(8),
        name="raw_order",
    )(raw_pulses.reshape(2, PULSES, 2048))
    own = jnp.concatenate([raw] + [flipped(raw, "y", mask) for mask in (1, 2, 3)], axis=0)
    other = flipped(own, "core", 1)

    rows = pl.pallas_call(
        copies_body,
        out_shape=jax.ShapeDtypeStruct((16, 2, 4, 1024), BF),
        in_specs=[LEFT],
        out_specs=LEFT,
        scratch_shapes=[pltpu.SemaphoreType.DMA((16,))],
        name="copies",
    )(range_filter)
    rows = exchange(rows, ALONG_Z)
    picked = pl.pallas_call(
        pick_body,
        out_shape=jax.ShapeDtypeStruct((4, ROW, COLS, 128), BF),
        in_specs=[WHOLE],
        out_specs=LEFT,
        scratch_shapes=[
            pltpu.VMEM((128, 1024), F32),
            pltpu.VMEM((ROW, COLS, 128), BF),
            pltpu.SemaphoreType.DMA((4, ROW)),
        ],
        compiler_params=params(8),
        name="pick_bins",
    )(rows)
    filters = exchange(picked.reshape(32, COLS, 128), PLANE)

    weights = band_weights.reshape(LEVELS, 2, 2, 2, ANG, BAND).transpose(0, 3, 1, 2, 5, 4)
    band = pl.pallas_call(
        band_body,
        grid=(2 * LEVELS,),
        out_shape=jax.ShapeDtypeStruct((2 * LEVELS, 2 * ANG, 2 * ANG), BF),
        in_specs=[
            pl.BlockSpec((1, 1, ANG), lambda i: (i, 0, 0)),
            pl.BlockSpec((1, 2, 2, BAND, ANG), lambda i: (i, 0, 0, 0, 0)),
        ],
        out_specs=pl.BlockSpec((1, 2 * ANG, 2 * ANG), lambda i: (i, 0, 0)),
        compiler_params=params(4),
        name="band",
    )(
        band_offsets.reshape(2 * LEVELS, 1, ANG),
        weights.reshape(2 * LEVELS, 2, 2, BAND, ANG),
    )

    filters, band = lax.optimization_barrier((filters, band))
    compressed = pl.pallas_call(
        compress_body,
        out_shape=jax.ShapeDtypeStruct((GROUP, SENT, 256), BF),
        in_specs=[WHOLE] * 3,
        out_specs=WHOLE,
        compiler_params=params(16),
        name="compress",
    )(filters, own, other)

    compressed, steer_angles, channel_mix = lax.optimization_barrier(
        (compressed, steer_angles, channel_mix)
    )
    offset = jnp.arange(ANG, dtype=jnp.int32).astype(F32) - 0.5 * ANG
    phase = steer_angles[None, :] * offset[:, None]
    factor = 1.0 / np.sqrt(ANG)
    beams = jnp.stack([jnp.cos(phase) * factor, jnp.sin(phase) * factor]).astype(BF)
    mix = channel_mix.transpose(0, 3, 2, 1).reshape(2, CHAN, 256)
    doppler = jnp.asarray(np.tile(doppler_table().transpose(0, 2, 1), (1, 1, CHAN)))
    operator = pl.pallas_call(
        operator_body,
        out_shape=jax.ShapeDtypeStruct((2, 256, 2 * ANG), BF),
        in_specs=[WHOLE] * 3,
        out_specs=WHOLE,
        compiler_params=params(8),
        name="operator",
    )(mix, doppler, beams)
    compressed = exchange(compressed, ("x0", "chan"))
    me = (lax.axis_index("y") * 2 + lax.axis_index("core")).astype(jnp.int32).reshape(1)
    power = pl.pallas_call(
        merge_body,
        out_shape=jax.ShapeDtypeStruct((GROUP, PAD, ANG), BF),
        in_specs=[SCALAR, WHOLE, WHOLE, LEFT],
        out_specs=WHOLE,
        scratch_shapes=[
            pltpu.VMEM((2, GROUP, PAD, 256), F32),
            pltpu.VMEM((2 * LEVELS, 2 * ANG, 2 * ANG), BF),
            pltpu.SemaphoreType.DMA((LEVELS,)),
        ],
        compiler_params=params(52),
        name="merge",
    )(me, compressed.reshape(GROUP * SENT, 256), operator, band)
    power = exchange(power, MERGE)
    chan = lax.axis_index("chan").astype(jnp.int32).reshape(1)
    return pl.pallas_call(
        despeckle_body,
        out_shape=jax.ShapeDtypeStruct((ANG, 128), F32),
        in_specs=[SCALAR] + [WHOLE] * 2,
        out_specs=WHOLE,
        scratch_shapes=[pltpu.VMEM((COLS, ANG), F32)],
        compiler_params=params(4),
        name="despeckle",
    )(chan, power, smoothing.reshape(1, ANG))


def solution(mesh):
    split = Mesh(mesh.devices.reshape(2, 2, 2, 4, 2, mesh.shape["chan"]), AXES)
    placed = (
        P(None, SUB, "chan", None),
        P(None, AXES, None),
        P(),
        P(),
        P(),
        P(),
        P(SUB),
    )
    return jax.shard_map(
        local, mesh=split, in_specs=placed, out_specs=P(SUB, "chan"), check_vma=False
    )
```

```python
import functools

import jax
import jax.numpy as jnp
import ml_dtypes
import numpy as np
from jax import lax
from jax.experimental import pallas as pl
from jax.experimental.pallas import tpu as pltpu
from jax.sharding import Mesh
from jax.sharding import PartitionSpec as P

ANG = 256
BAND = 8
LEVELS = 4
PASSES = 3
PULSES = 32
CHAN = 8
GROUP = 16
ROW = 8
CUT = 9
PAD = 16
SENT = 24
HALO = 8
COLS = GROUP * CUT
REVERSED = [8 * (m & 1) + 4 * (m >> 1 & 1) + 2 * (m >> 2 & 1) + (m >> 3) for m in range(GROUP)]
AXES = ("zh", "x1", "x0", "y", "core", "chan")
SUB = ("zh", "x1", "x0", "y", "core")
ALONG_Z = ("zh", "chan")
PLANE = ("x1", "x0", "y", "core")
MERGE = ("x0", "y", "core")
BF = jnp.bfloat16
F32 = jnp.float32
WHOLE = pl.BlockSpec(memory_space=pltpu.VMEM)
LEFT = pl.BlockSpec(memory_space=pltpu.HBM)
SCALAR = pl.BlockSpec(memory_space=pltpu.SMEM)


def params(mib):
    return pltpu.CompilerParams(vmem_limit_bytes=mib << 20)


def iota(shape, dim):
    return lax.broadcasted_iota(jnp.int32, shape, dim)


def dot(left, right):
    return jnp.dot(left, right, preferred_element_type=F32)


def dot_t(left, right):
    return lax.dot_general(left, right, (((1,), (1,)), ((), ())), preferred_element_type=F32)


def raw_body(raw_ref, out_ref):
    row, col = iota((512, 512), 0), iota((512, 512), 1)
    quarter, part, half, k = col >> 7, (col >> 6) & 1, (col >> 5) & 1, col & 31
    source = part * 256 + half * 128 + quarter * 32 + k
    sign = jnp.where(part == 1, -1.0, 1.0)
    order = jnp.where(row == source, sign, 0.0).astype(BF)
    rows = []
    for u in range(8):
        rows.append(
            jnp.concatenate(
                [
                    raw_ref[part, :, half * 1024 + u * 128 : half * 1024 + (u + 1) * 128]
                    for part in range(2)
                    for half in range(2)
                ],
                axis=1,
            )
        )
    moved = dot(jnp.concatenate(rows, axis=0), order).astype(BF)
    for u in range(8):
        out_ref[:, u * 512 : (u + 1) * 512] = moved[u * 32 : (u + 1) * 32]


def pick_body(filter_ref, out_far, ordered, picked, sems):
    for z in range(16):
        for part in range(2):
            at = part * 64 + z * 4
            ordered[at : at + 4, :] = filter_ref[z, part].astype(F32)
    rows = ordered[...].astype(BF)
    bins = iota((COLS, 1024), 1)
    r = iota((COLS, 1024), 0)
    dest = r // CUT
    first = 128 * (dest & 7) - HALO + 8 * CUT * (dest >> 3) + r - dest * CUT
    copies = []
    for g in range(ROW):
        pick = jnp.where(bins == first + CUT * g, 1.0, 0.0).astype(BF)
        picked[g] = dot_t(pick, rows).astype(BF)
        for x in range(4):
            copy = pltpu.make_async_copy(picked.at[g], out_far.at[x, g], sems.at[x, g])
            copy.start()
            copies.append(copy)
    for copy in copies:
        copy.wait()


def compress_body(filter_ref, own_ref, other_ref, out_ref, pulses):
    pulses[:128, :] = own_ref[...]
    pulses[128:, :] = other_ref[...]
    first, second = [], []
    for s in range(32):
        block = filter_ref[s]
        first.append(block)
        second.append(jnp.concatenate([block[:, 64:], -block[:, :64]], axis=1))
    left = jnp.concatenate(
        [jnp.concatenate(first, axis=1), jnp.concatenate(second, axis=1)], axis=0
    )
    summed = dot_t(left, pulses[...])
    row, col = iota((32 * GROUP, 2 * COLS), 0), iota((32 * GROUP, 2 * COLS), 1)
    within = row & 31
    source = (row >> 5) * CUT + jnp.where(within >= CUT, within - CUT + COLS, within)
    order = jnp.where((col == source) & (within < 2 * CUT), 1.0, 0.0).astype(BF)
    moved = dot(order, summed.astype(BF)).astype(BF)
    for dest in range(GROUP):
        out_ref[dest] = moved[dest * 32 : dest * 32 + SENT]


def operator_body(mix_ref, dop_ref, beam_ref, out_ref):
    real, imag = [], []
    for c in range(CHAN):
        mr, mi = mix_ref[0, c : c + 1, :], mix_ref[1, c : c + 1, :]
        real.append(mr * dop_ref[0] - mi * dop_ref[1])
        imag.append(mr * dop_ref[1] + mi * dop_ref[0])
    both = jnp.concatenate(real + imag, axis=0)
    top = both.astype(BF)
    rest = (both - top.astype(F32)).astype(BF)
    by_real = dot(top, beam_ref[0]) + dot(rest, beam_ref[0])
    by_imag = dot(top, beam_ref[1]) + dot(rest, beam_ref[1])
    whole = jnp.concatenate(
        [by_real[:256] - by_imag[256:], by_real[256:] + by_imag[:256]], axis=1
    )
    top = whole.astype(BF)
    out_ref[0] = top
    out_ref[1] = (whole - top.astype(F32)).astype(BF)


def band_body(offset_ref, weight_ref, out_ref):
    strip = 32
    offset = jnp.broadcast_to(offset_ref[0], (strip, ANG))
    for start in range(0, ANG, strip):
        step = iota((strip, ANG), 0) + start - offset
        hits = [step == j for j in range(BAND)]
        for c in range(2):
            for part in range(2):
                value = jnp.zeros((strip, ANG), F32)
                for j in range(BAND):
                    value = jnp.where(hits[j], weight_ref[0, c, part, j : j + 1, :], value)
                out_ref[
                    0, c * ANG + start : c * ANG + start + strip, part * ANG : (part + 1) * ANG
                ] = value.astype(BF)


def merge_body(me_ref, comp_ref, operator_ref, band_far, out_ref, pulses, band, sems):
    copies = []
    for level in range(LEVELS):
        span = slice(2 * level, 2 * level + 2)
        copies.append(pltpu.make_async_copy(band_far.at[span], band.at[span], sems.at[level]))
    for copy in copies:
        copy.start()
    me = me_ref[0]
    apart = comp_ref[...].astype(F32)
    for x in range(2):
        for part in range(2):
            blocks = []
            for c in range(CHAN):
                at = (x * 8 + c) * SENT + part * CUT
                blocks.append(apart[at : at + CUT])
            for q in range(8):
                n = x * 8 + (((q & 3) * 2 + (q >> 2)) ^ me)
                pulses[part, n, :CUT, :] = jnp.concatenate(
                    [b[:, q * 32 : (q + 1) * 32] for b in blocks], axis=1
                )
    pulse = pulses[...].reshape(2 * GROUP * PAD, 256).astype(BF)
    formed = dot(pulse, operator_ref[0]) + dot(pulse, operator_ref[1])
    half = GROUP * PAD
    real = formed[:half, :ANG] - formed[half:, ANG:]
    imag = formed[half:, :ANG] + formed[:half, ANG:]
    real, imag = [
        jnp.concatenate([part[n * PAD : n * PAD + CUT] for n in REVERSED], axis=0)
        for part in (real, imag)
    ]
    half = COLS // 2
    for level in range(LEVELS):
        block = COLS >> level
        sides = []
        for c in range(2):
            starts = [k * block + c * (block // 2) for k in range(1 << level)]
            sides.append(
                jnp.concatenate(
                    [part[at : at + block // 2] for part in (real, imag) for at in starts], axis=0
                )
            )
        left = jnp.concatenate(sides, axis=1)
        top = left.astype(BF)
        rest = (left - top.astype(F32)).astype(BF)
        reals, imags = [], []
        copies[level].wait()
        for h in range(2):
            weight = band[2 * level + h]
            out = dot(top, weight) + dot(rest, weight)
            reals.append(out[:half, :ANG] - out[half:, ANG:])
            imags.append(out[half:, :ANG] + out[:half, ANG:])
        real = jnp.concatenate(reals, axis=0)
        imag = jnp.concatenate(imags, axis=0)
    power = real * real + imag * imag
    rest = jnp.zeros((PAD - CUT, ANG), F32)
    for n in range(GROUP):
        out_ref[n] = jnp.concatenate([power[n * CUT : (n + 1) * CUT], rest], axis=0).astype(BF)


def despeckle_body(chan_ref, power_ref, rate_ref, out_ref, bins):
    for t in range(GROUP):
        bins[t * CUT : (t + 1) * CUT, :] = power_ref[t].astype(F32)[:CUT]
    current = bins[...]
    cell = iota((COLS, ANG), 0) + (chan_ref[0] * 128 - HALO)
    inside = (cell >= 0) & (cell < 1024)
    rate = jnp.broadcast_to(rate_ref[...], (COLS, ANG))
    for _ in range(PASSES):
        before = pltpu.roll(current, 1, 0)
        after = pltpu.roll(current, COLS - 1, 0)
        current = jnp.where(inside, current + rate * (before - 2.0 * current + after), 0.0)
    out_ref[...] = current[HALO : HALO + 128, :].T


def doppler_table():
    index = np.arange(PULSES)
    phase = np.float32(2.0 * np.pi / PULSES) * (
        index[:, None] * index[None, :] % PULSES
    ).astype(np.float32)
    factor = np.float32(1.0 / np.sqrt(PULSES))
    parts = np.stack([np.cos(phase) * factor, -np.sin(phase) * factor])
    return parts.astype(ml_dtypes.bfloat16).astype(np.float32)


def flipped(value, axis, mask):
    pairs = [(source, source ^ mask) for source in range(lax.axis_size(axis))]
    return lax.ppermute(value, axis, pairs)


def exchange(value, axes):
    return lax.all_to_all(value, axes, split_axis=0, concat_axis=0, tiled=True)


def local(
    raw_pulses, range_filter, channel_mix, steer_angles, band_offsets, band_weights, smoothing
):
    raw = pl.pallas_call(
        raw_body,
        out_shape=jax.ShapeDtypeStruct((PULSES, 4096), BF),
        in_specs=[WHOLE],
        out_specs=WHOLE,
        compiler_params=params(8),
        name="raw_order",
    )(raw_pulses.reshape(2, PULSES, 2048))
    own = jnp.concatenate([raw] + [flipped(raw, "y", mask) for mask in (1, 2, 3)], axis=0)
    other = flipped(own, "core", 1)

    rows = jnp.broadcast_to(range_filter[None], (16, *range_filter.shape))
    rows = exchange(rows, ALONG_Z)
    picked = pl.pallas_call(
        pick_body,
        out_shape=jax.ShapeDtypeStruct((4, ROW, COLS, 128), BF),
        in_specs=[WHOLE],
        out_specs=LEFT,
        scratch_shapes=[
            pltpu.VMEM((128, 1024), F32),
            pltpu.VMEM((ROW, COLS, 128), BF),
            pltpu.SemaphoreType.DMA((4, ROW)),
        ],
        compiler_params=params(8),
        name="pick_bins",
    )(rows)
    filters = exchange(picked.reshape(32, COLS, 128), PLANE)

    weights = band_weights.reshape(LEVELS, 2, 2, 2, ANG, BAND).transpose(0, 3, 1, 2, 5, 4)
    band = pl.pallas_call(
        band_body,
        grid=(2 * LEVELS,),
        out_shape=jax.ShapeDtypeStruct((2 * LEVELS, 2 * ANG, 2 * ANG), BF),
        in_specs=[
            pl.BlockSpec((1, 1, ANG), lambda i: (i, 0, 0)),
            pl.BlockSpec((1, 2, 2, BAND, ANG), lambda i: (i, 0, 0, 0, 0)),
        ],
        out_specs=pl.BlockSpec((1, 2 * ANG, 2 * ANG), lambda i: (i, 0, 0)),
        compiler_params=params(4),
        name="band",
    )(
        band_offsets.reshape(2 * LEVELS, 1, ANG),
        weights.reshape(2 * LEVELS, 2, 2, BAND, ANG),
    )

    filters, band = lax.optimization_barrier((filters, band))
    compressed = pl.pallas_call(
        compress_body,
        out_shape=jax.ShapeDtypeStruct((GROUP, SENT, 256), BF),
        in_specs=[WHOLE] * 3,
        out_specs=WHOLE,
        scratch_shapes=[pltpu.VMEM((256, 4096), BF)],
        compiler_params=params(16),
        name="compress",
    )(filters, own, other)

    compressed, steer_angles, channel_mix = lax.optimization_barrier(
        (compressed, steer_angles, channel_mix)
    )
    offset = jnp.arange(ANG, dtype=jnp.int32).astype(F32) - 0.5 * ANG
    phase = steer_angles[None, :] * offset[:, None]
    factor = 1.0 / np.sqrt(ANG)
    beams = jnp.stack([jnp.cos(phase) * factor, jnp.sin(phase) * factor]).astype(BF)
    mix = channel_mix.transpose(0, 3, 2, 1).reshape(2, CHAN, 256)
    doppler = jnp.asarray(np.tile(doppler_table().transpose(0, 2, 1), (1, 1, CHAN)))
    operator = pl.pallas_call(
        operator_body,
        out_shape=jax.ShapeDtypeStruct((2, 256, 2 * ANG), BF),
        in_specs=[WHOLE] * 3,
        out_specs=WHOLE,
        compiler_params=params(8),
        name="operator",
    )(mix, doppler, beams)
    compressed = exchange(compressed, ("x0", "chan"))
    me = (lax.axis_index("y") * 2 + lax.axis_index("core")).astype(jnp.int32).reshape(1)
    power = pl.pallas_call(
        merge_body,
        out_shape=jax.ShapeDtypeStruct((GROUP, PAD, ANG), BF),
        in_specs=[SCALAR, WHOLE, WHOLE, LEFT],
        out_specs=WHOLE,
        scratch_shapes=[
            pltpu.VMEM((2, GROUP, PAD, 256), F32),
            pltpu.VMEM((2 * LEVELS, 2 * ANG, 2 * ANG), BF),
            pltpu.SemaphoreType.DMA((LEVELS,)),
        ],
        compiler_params=params(52),
        name="merge",
    )(me, compressed.reshape(GROUP * SENT, 256), operator, band)
    power = exchange(power, MERGE)
    chan = lax.axis_index("chan").astype(jnp.int32).reshape(1)
    return pl.pallas_call(
        despeckle_body,
        out_shape=jax.ShapeDtypeStruct((ANG, 128), F32),
        in_specs=[SCALAR] + [WHOLE] * 2,
        out_specs=WHOLE,
        scratch_shapes=[pltpu.VMEM((COLS, ANG), F32)],
        compiler_params=params(4),
        name="despeckle",
    )(chan, power, smoothing.reshape(1, ANG))


def solution(mesh):
    split = Mesh(mesh.devices.reshape(2, 2, 2, 4, 2, mesh.shape["chan"]), AXES)
    placed = (
        P(None, SUB, "chan", None),
        P(None, AXES, None),
        P(),
        P(),
        P(),
        P(),
        P(SUB),
    )
    return jax.shard_map(
        local, mesh=split, in_specs=placed, out_specs=P(SUB, "chan"), check_vma=False
    )
```

```python
import functools

import jax
import jax.numpy as jnp
import ml_dtypes
import numpy as np
from jax import lax
from jax.experimental import pallas as pl
from jax.experimental.pallas import tpu as pltpu
from jax.sharding import Mesh
from jax.sharding import PartitionSpec as P

ANG = 256
BAND = 8
LEVELS = 4
PASSES = 3
PULSES = 32
CHAN = 8
GROUP = 16
ROW = 8
CUT = 9
PAD = 16
SENT = 40
HALO = 4
COLS = GROUP * CUT
LOWER = 8 * CUT
PICKED = LOWER + 64
REVERSED = [8 * (m & 1) + 4 * (m >> 1 & 1) + 2 * (m >> 2 & 1) + (m >> 3) for m in range(GROUP)]
AXES = ("zh", "x1", "x0", "y", "core", "chan")
SUB = ("zh", "x1", "x0", "y", "core")
ALONG_Z = ("zh", "chan")
PLANE = ("x1", "x0", "y", "core")
MERGE = ("x0", "y", "core")
BF = jnp.bfloat16
F32 = jnp.float32
WHOLE = pl.BlockSpec(memory_space=pltpu.VMEM)
LEFT = pl.BlockSpec(memory_space=pltpu.HBM)
SCALAR = pl.BlockSpec(memory_space=pltpu.SMEM)


def params(mib):
    return pltpu.CompilerParams(vmem_limit_bytes=mib << 20)


def iota(shape, dim):
    return lax.broadcasted_iota(jnp.int32, shape, dim)


def dot(left, right):
    return jnp.dot(left, right, preferred_element_type=F32)


def dot_t(left, right):
    return lax.dot_general(left, right, (((1,), (1,)), ((), ())), preferred_element_type=F32)


def raw_body(raw_ref, out_ref):
    row, col = iota((512, 512), 0), iota((512, 512), 1)
    quarter, part, half, k = col >> 7, (col >> 6) & 1, (col >> 5) & 1, col & 31
    source = part * 256 + half * 128 + quarter * 32 + k
    sign = jnp.where(part == 1, -1.0, 1.0)
    order = jnp.where(row == source, sign, 0.0).astype(BF)
    rows = []
    for u in range(8):
        rows.append(
            jnp.concatenate(
                [
                    raw_ref[part, :, half * 1024 + u * 128 : half * 1024 + (u + 1) * 128]
                    for part in range(2)
                    for half in range(2)
                ],
                axis=1,
            )
        )
    moved = dot(jnp.concatenate(rows, axis=0), order).astype(BF)
    for u in range(8):
        out_ref[:, u * 512 : (u + 1) * 512] = moved[u * 32 : (u + 1) * 32]


def pick_body(filter_ref, out_far, ordered, picked, sems):
    for z in range(16):
        for part in range(2):
            at = part * 64 + z * 4
            ordered[at : at + 4, :] = filter_ref[z, part].astype(F32)
    rows = ordered[...].astype(BF)
    r, k = iota((LOWER, 1024), 0), iota((64, 1024), 0)
    dest = r // CUT
    lower = iota((LOWER, 1024), 1) - (128 * dest - HALO + r - dest * CUT)
    upper = iota((64, 1024), 1) - (128 * (k >> 3) - HALO + LOWER + (k & 7))
    copies = []
    for g in range(ROW):
        hits = [jnp.where(lower == CUT * g, 1.0, 0.0), jnp.where(upper == 8 * g, 1.0, 0.0)]
        pick = jnp.concatenate(hits, axis=0).astype(BF)
        picked[g] = dot_t(pick, rows).astype(BF)
        for x in range(4):
            copy = pltpu.make_async_copy(picked.at[g], out_far.at[x, g], sems.at[x, g])
            copy.start()
            copies.append(copy)
    for copy in copies:
        copy.wait()


def compress_body(filter_ref, own_ref, other_ref, out_ref, pulses):
    pulses[:128, :] = own_ref[...]
    pulses[128:, :] = other_ref[...]
    first, second = [], []
    for s in range(32):
        block = filter_ref[s]
        first.append(block)
        second.append(jnp.concatenate([block[:, 64:], -block[:, :64]], axis=1))
    left = jnp.concatenate(
        [jnp.concatenate(first, axis=1), jnp.concatenate(second, axis=1)], axis=0
    )
    summed = dot_t(left, pulses[...])
    row, col = iota((32 * GROUP, 2 * PICKED), 0), iota((32 * GROUP, 2 * PICKED), 1)
    within = row & 31
    j = jnp.where(within >= CUT, within - CUT, within)
    c = (row >> 5) & 7
    upper = row >= 8 * 32
    source = jnp.where(upper, LOWER + 8 * c, CUT * c) + j
    source = jnp.where(within >= CUT, source + PICKED, source)
    held = (within < 2 * CUT) & ((j < 8) | ~upper)
    order = jnp.where((col == source) & held, 1.0, 0.0).astype(BF)
    moved = dot(order, summed.astype(BF))
    rest = jnp.zeros((SENT - 4 * CUT, 128), F32)
    for dest in range(GROUP):
        block = moved[dest * 32 : dest * 32 + 2 * CUT]
        out_ref[dest] = jnp.concatenate([block[:, :128], block[:, 128:], rest], axis=0).astype(BF)


def operator_body(mix_ref, dop_ref, beam_ref, out_ref):
    real, imag = [], []
    for c in range(CHAN):
        mr, mi = mix_ref[0, c : c + 1, :], mix_ref[1, c : c + 1, :]
        real.append(mr * dop_ref[0] - mi * dop_ref[1])
        imag.append(mr * dop_ref[1] + mi * dop_ref[0])
    both = jnp.concatenate(real + imag, axis=0)
    top = both.astype(BF)
    rest = (both - top.astype(F32)).astype(BF)
    by_real = dot(top, beam_ref[0]) + dot(rest, beam_ref[0])
    by_imag = dot(top, beam_ref[1]) + dot(rest, beam_ref[1])
    whole = jnp.concatenate(
        [by_real[:256] - by_imag[256:], by_real[256:] + by_imag[:256]], axis=1
    )
    top = whole.astype(BF)
    out_ref[0] = top
    out_ref[1] = (whole - top.astype(F32)).astype(BF)


def band_body(offset_ref, weight_ref, out_ref):
    strip = 32
    offset = jnp.broadcast_to(offset_ref[0], (strip, ANG))
    for start in range(0, ANG, strip):
        step = iota((strip, ANG), 0) + start - offset
        hits = [step == j for j in range(BAND)]
        for c in range(2):
            for part in range(2):
                value = jnp.zeros((strip, ANG), F32)
                for j in range(BAND):
                    value = jnp.where(hits[j], weight_ref[0, c, part, j : j + 1, :], value)
                out_ref[
                    0, c * ANG + start : c * ANG + start + strip, part * ANG : (part + 1) * ANG
                ] = value.astype(BF)


def merge_body(me_ref, comp_ref, operator_ref, band_far, out_ref, pulses, band, sems):
    copies = []
    for level in range(LEVELS):
        span = slice(2 * level, 2 * level + 2)
        copies.append(pltpu.make_async_copy(band_far.at[span], band.at[span], sems.at[level]))
    for copy in copies:
        copy.start()
    me = me_ref[0]
    apart = comp_ref[...].astype(F32)
    for x in range(2):
        for part in range(2):
            for q in range(8):
                n = x * 8 + (((q & 3) * 2 + (q >> 2)) ^ me)
                blocks = []
                for c in range(CHAN):
                    at = (x * 8 + c) * SENT + (q >> 2) * 2 * CUT + part * CUT
                    blocks.append(apart[at : at + CUT, (q & 3) * 32 : (q & 3) * 32 + 32])
                pulses[part, n, :CUT, :] = jnp.concatenate(blocks, axis=1)
    pulse = pulses[...].reshape(2 * GROUP * PAD, 256).astype(BF)
    formed = dot(pulse, operator_ref[0]) + dot(pulse, operator_ref[1])
    half = GROUP * PAD
    real = formed[:half, :ANG] - formed[half:, ANG:]
    imag = formed[half:, :ANG] + formed[:half, ANG:]
    real, imag = [
        jnp.concatenate([part[n * PAD : n * PAD + CUT] for n in REVERSED], axis=0)
        for part in (real, imag)
    ]
    half = COLS // 2
    for level in range(LEVELS):
        block = COLS >> level
        sides = []
        for c in range(2):
            starts = [k * block + c * (block // 2) for k in range(1 << level)]
            sides.append(
                jnp.concatenate(
                    [part[at : at + block // 2] for part in (real, imag) for at in starts], axis=0
                )
            )
        left = jnp.concatenate(sides, axis=1)
        top = left.astype(BF)
        rest = (left - top.astype(F32)).astype(BF)
        reals, imags = [], []
        copies[level].wait()
        for h in range(2):
            weight = band[2 * level + h]
            out = dot(top, weight) + dot(rest, weight)
            reals.append(out[:half, :ANG] - out[half:, ANG:])
            imags.append(out[half:, :ANG] + out[:half, ANG:])
        real = jnp.concatenate(reals, axis=0)
        imag = jnp.concatenate(imags, axis=0)
    power = real * real + imag * imag
    rest = jnp.zeros((PAD - CUT, ANG), F32)
    for n in range(GROUP):
        out_ref[n] = jnp.concatenate([power[n * CUT : (n + 1) * CUT], rest], axis=0).astype(BF)


def despeckle_body(chan_ref, power_ref, rate_ref, out_ref, bins):
    for t in range(GROUP):
        at, count = (t * CUT, CUT) if t < 8 else (LOWER + (t - 8) * 8, 8)
        bins[at : at + count, :] = power_ref[t].astype(F32)[:count]
    current = bins[...]
    cell = iota((PICKED, ANG), 0) + (chan_ref[0] * 128 - HALO)
    inside = (cell >= 0) & (cell < 1024)
    rate = jnp.broadcast_to(rate_ref[...], (PICKED, ANG))
    for _ in range(PASSES):
        before = pltpu.roll(current, 1, 0)
        after = pltpu.roll(current, PICKED - 1, 0)
        current = jnp.where(inside, current + rate * (before - 2.0 * current + after), 0.0)
    out_ref[...] = current[HALO : HALO + 128, :].T


def doppler_table():
    index = np.arange(PULSES)
    phase = np.float32(2.0 * np.pi / PULSES) * (
        index[:, None] * index[None, :] % PULSES
    ).astype(np.float32)
    factor = np.float32(1.0 / np.sqrt(PULSES))
    parts = np.stack([np.cos(phase) * factor, -np.sin(phase) * factor])
    return parts.astype(ml_dtypes.bfloat16).astype(np.float32)


def flipped(value, axis, mask):
    pairs = [(source, source ^ mask) for source in range(lax.axis_size(axis))]
    return lax.ppermute(value, axis, pairs)


def exchange(value, axes):
    return lax.all_to_all(value, axes, split_axis=0, concat_axis=0, tiled=True)


def local(
    raw_pulses, range_filter, channel_mix, steer_angles, band_offsets, band_weights, smoothing
):
    raw = pl.pallas_call(
        raw_body,
        out_shape=jax.ShapeDtypeStruct((PULSES, 4096), BF),
        in_specs=[WHOLE],
        out_specs=WHOLE,
        compiler_params=params(8),
        name="raw_order",
    )(raw_pulses.reshape(2, PULSES, 2048))
    own = jnp.concatenate([raw] + [flipped(raw, "y", mask) for mask in (1, 2, 3)], axis=0)
    other = flipped(own, "core", 1)

    rows = jnp.broadcast_to(range_filter[None], (16, *range_filter.shape))
    rows = exchange(rows, ALONG_Z)
    picked = pl.pallas_call(
        pick_body,
        out_shape=jax.ShapeDtypeStruct((4, ROW, PICKED, 128), BF),
        in_specs=[WHOLE],
        out_specs=LEFT,
        scratch_shapes=[
            pltpu.VMEM((128, 1024), F32),
            pltpu.VMEM((ROW, PICKED, 128), BF),
            pltpu.SemaphoreType.DMA((4, ROW)),
        ],
        compiler_params=params(8),
        name="pick_bins",
    )(rows)
    filters = exchange(picked.reshape(32, PICKED, 128), PLANE)

    weights = band_weights.reshape(LEVELS, 2, 2, 2, ANG, BAND).transpose(0, 3, 1, 2, 5, 4)
    band = pl.pallas_call(
        band_body,
        grid=(2 * LEVELS,),
        out_shape=jax.ShapeDtypeStruct((2 * LEVELS, 2 * ANG, 2 * ANG), BF),
        in_specs=[
            pl.BlockSpec((1, 1, ANG), lambda i: (i, 0, 0)),
            pl.BlockSpec((1, 2, 2, BAND, ANG), lambda i: (i, 0, 0, 0, 0)),
        ],
        out_specs=pl.BlockSpec((1, 2 * ANG, 2 * ANG), lambda i: (i, 0, 0)),
        compiler_params=params(4),
        name="band",
    )(
        band_offsets.reshape(2 * LEVELS, 1, ANG),
        weights.reshape(2 * LEVELS, 2, 2, BAND, ANG),
    )

    filters, band = lax.optimization_barrier((filters, band))
    compressed = pl.pallas_call(
        compress_body,
        out_shape=jax.ShapeDtypeStruct((GROUP, SENT, 128), BF),
        in_specs=[WHOLE] * 3,
        out_specs=WHOLE,
        scratch_shapes=[pltpu.VMEM((256, 4096), BF)],
        compiler_params=params(16),
        name="compress",
    )(filters, own, other)

    compressed, steer_angles, channel_mix = lax.optimization_barrier(
        (compressed, steer_angles, channel_mix)
    )
    offset = jnp.arange(ANG, dtype=jnp.int32).astype(F32) - 0.5 * ANG
    phase = steer_angles[None, :] * offset[:, None]
    factor = 1.0 / np.sqrt(ANG)
    beams = jnp.stack([jnp.cos(phase) * factor, jnp.sin(phase) * factor]).astype(BF)
    mix = channel_mix.transpose(0, 3, 2, 1).reshape(2, CHAN, 256)
    doppler = jnp.asarray(np.tile(doppler_table().transpose(0, 2, 1), (1, 1, CHAN)))
    operator = pl.pallas_call(
        operator_body,
        out_shape=jax.ShapeDtypeStruct((2, 256, 2 * ANG), BF),
        in_specs=[WHOLE] * 3,
        out_specs=WHOLE,
        compiler_params=params(8),
        name="operator",
    )(mix, doppler, beams)
    compressed = exchange(compressed, ("x0", "chan"))
    me = (lax.axis_index("y") * 2 + lax.axis_index("core")).astype(jnp.int32).reshape(1)
    power = pl.pallas_call(
        merge_body,
        out_shape=jax.ShapeDtypeStruct((GROUP, PAD, ANG), BF),
        in_specs=[SCALAR, WHOLE, WHOLE, LEFT],
        out_specs=WHOLE,
        scratch_shapes=[
            pltpu.VMEM((2, GROUP, PAD, 256), F32),
            pltpu.VMEM((2 * LEVELS, 2 * ANG, 2 * ANG), BF),
            pltpu.SemaphoreType.DMA((LEVELS,)),
        ],
        compiler_params=params(52),
        name="merge",
    )(me, compressed.reshape(GROUP * SENT, 128), operator, band)
    power = exchange(power, MERGE)
    chan = lax.axis_index("chan").astype(jnp.int32).reshape(1)
    return pl.pallas_call(
        despeckle_body,
        out_shape=jax.ShapeDtypeStruct((ANG, 128), F32),
        in_specs=[SCALAR] + [WHOLE] * 2,
        out_specs=WHOLE,
        scratch_shapes=[pltpu.VMEM((PICKED, ANG), F32)],
        compiler_params=params(4),
        name="despeckle",
    )(chan, power, smoothing.reshape(1, ANG))


def solution(mesh):
    split = Mesh(mesh.devices.reshape(2, 2, 2, 4, 2, mesh.shape["chan"]), AXES)
    placed = (
        P(None, SUB, "chan", None),
        P(None, AXES, None),
        P(),
        P(),
        P(),
        P(),
        P(SUB),
    )
    return jax.shard_map(
        local, mesh=split, in_specs=placed, out_specs=P(SUB, "chan"), check_vma=False
    )
```

```python
import functools

import jax
import jax.numpy as jnp
import ml_dtypes
import numpy as np
from jax import lax
from jax.experimental import pallas as pl
from jax.experimental.pallas import tpu as pltpu
from jax.sharding import Mesh
from jax.sharding import PartitionSpec as P

ANG = 256
BAND = 8
LEVELS = 4
PASSES = 3
PULSES = 32
CHAN = 8
GROUP = 16
ROW = 8
CUT = 9
PAD = 16
SENT = 40
HALO = 4
COLS = GROUP * CUT
LOWER = 8 * CUT
PICKED = LOWER + 64
REVERSED = [8 * (m & 1) + 4 * (m >> 1 & 1) + 2 * (m >> 2 & 1) + (m >> 3) for m in range(GROUP)]
AXES = ("zh", "x1", "x0", "y", "core", "chan")
SUB = ("zh", "x1", "x0", "y", "core")
ALONG_Z = ("zh", "chan")
PLANE = ("x1", "x0", "y", "core")
MERGE = ("x0", "y", "core")
BF = jnp.bfloat16
F32 = jnp.float32
WHOLE = pl.BlockSpec(memory_space=pltpu.VMEM)
LEFT = pl.BlockSpec(memory_space=pltpu.HBM)
SCALAR = pl.BlockSpec(memory_space=pltpu.SMEM)


def params(mib):
    return pltpu.CompilerParams(vmem_limit_bytes=mib << 20)


def iota(shape, dim):
    return lax.broadcasted_iota(jnp.int32, shape, dim)


def dot(left, right):
    return jnp.dot(left, right, preferred_element_type=F32)


def dot_t(left, right):
    return lax.dot_general(left, right, (((1,), (1,)), ((), ())), preferred_element_type=F32)


def raw_body(raw_ref, out_ref):
    row, col = iota((512, 512), 0), iota((512, 512), 1)
    quarter, part, half, k = col >> 7, (col >> 6) & 1, (col >> 5) & 1, col & 31
    source = part * 256 + half * 128 + quarter * 32 + k
    sign = jnp.where(part == 1, -1.0, 1.0)
    order = jnp.where(row == source, sign, 0.0).astype(BF)
    rows = []
    for u in range(8):
        rows.append(
            jnp.concatenate(
                [
                    raw_ref[part, :, half * 1024 + u * 128 : half * 1024 + (u + 1) * 128]
                    for part in range(2)
                    for half in range(2)
                ],
                axis=1,
            )
        )
    moved = dot(jnp.concatenate(rows, axis=0), order).astype(BF)
    for u in range(8):
        out_ref[:, u * 512 : (u + 1) * 512] = moved[u * 32 : (u + 1) * 32]


def copies_body(filter_far, out_far, rows, sem, sems):
    first = pltpu.make_async_copy(filter_far, rows, sem)
    first.start()
    first.wait()
    copies = [pltpu.make_async_copy(rows, out_far.at[z], sems.at[z]) for z in range(16)]
    for copy in copies:
        copy.start()
    for copy in copies:
        copy.wait()


def pick_body(filter_ref, out_far, ordered, picked, sems):
    for z in range(16):
        for part in range(2):
            at = part * 64 + z * 4
            ordered[at : at + 4, :] = filter_ref[z, part].astype(F32)
    rows = ordered[...].astype(BF)
    r, k = iota((LOWER, 1024), 0), iota((64, 1024), 0)
    dest = r // CUT
    lower = iota((LOWER, 1024), 1) - (128 * dest - HALO + r - dest * CUT)
    upper = iota((64, 1024), 1) - (128 * (k >> 3) - HALO + LOWER + (k & 7))
    copies = []
    for g in range(ROW):
        hits = [jnp.where(lower == CUT * g, 1.0, 0.0), jnp.where(upper == 8 * g, 1.0, 0.0)]
        pick = jnp.concatenate(hits, axis=0).astype(BF)
        picked[g] = dot_t(pick, rows).astype(BF)
        for x in range(4):
            copy = pltpu.make_async_copy(picked.at[g], out_far.at[x, g], sems.at[x, g])
            copy.start()
            copies.append(copy)
    for copy in copies:
        copy.wait()


def compress_body(filter_ref, own_ref, other_ref, out_ref, pulses):
    pulses[:128, :] = own_ref[...]
    pulses[128:, :] = other_ref[...]
    first, second = [], []
    for s in range(32):
        block = filter_ref[s]
        first.append(block)
        second.append(jnp.concatenate([block[:, 64:], -block[:, :64]], axis=1))
    left = jnp.concatenate(
        [jnp.concatenate(first, axis=1), jnp.concatenate(second, axis=1)], axis=0
    )
    summed = dot_t(left, pulses[...])
    row, col = iota((32 * GROUP, 2 * PICKED), 0), iota((32 * GROUP, 2 * PICKED), 1)
    within = row & 31
    j = jnp.where(within >= CUT, within - CUT, within)
    c = (row >> 5) & 7
    upper = row >= 8 * 32
    source = jnp.where(upper, LOWER + 8 * c, CUT * c) + j
    source = jnp.where(within >= CUT, source + PICKED, source)
    held = (within < 2 * CUT) & ((j < 8) | ~upper)
    order = jnp.where((col == source) & held, 1.0, 0.0).astype(BF)
    moved = dot(order, summed.astype(BF))
    rest = jnp.zeros((SENT - 4 * CUT, 128), F32)
    for dest in range(GROUP):
        block = moved[dest * 32 : dest * 32 + 2 * CUT]
        out_ref[dest] = jnp.concatenate([block[:, :128], block[:, 128:], rest], axis=0).astype(BF)


def operator_body(mix_ref, dop_ref, beam_ref, out_ref):
    real, imag = [], []
    for c in range(CHAN):
        mr, mi = mix_ref[0, c : c + 1, :], mix_ref[1, c : c + 1, :]
        real.append(mr * dop_ref[0] - mi * dop_ref[1])
        imag.append(mr * dop_ref[1] + mi * dop_ref[0])
    both = jnp.concatenate(real + imag, axis=0)
    top = both.astype(BF)
    rest = (both - top.astype(F32)).astype(BF)
    by_real = dot(top, beam_ref[0]) + dot(rest, beam_ref[0])
    by_imag = dot(top, beam_ref[1]) + dot(rest, beam_ref[1])
    whole = jnp.concatenate(
        [by_real[:256] - by_imag[256:], by_real[256:] + by_imag[:256]], axis=1
    )
    top = whole.astype(BF)
    out_ref[0] = top
    out_ref[1] = (whole - top.astype(F32)).astype(BF)


def band_body(offset_ref, weight_ref, out_ref):
    strip = 32
    offset = jnp.broadcast_to(offset_ref[0], (strip, ANG))
    for start in range(0, ANG, strip):
        step = iota((strip, ANG), 0) + start - offset
        hits = [step == j for j in range(BAND)]
        for c in range(2):
            for part in range(2):
                value = jnp.zeros((strip, ANG), F32)
                for j in range(BAND):
                    value = jnp.where(hits[j], weight_ref[0, c, part, j : j + 1, :], value)
                out_ref[
                    0, c * ANG + start : c * ANG + start + strip, part * ANG : (part + 1) * ANG
                ] = value.astype(BF)


def merge_body(me_ref, comp_ref, operator_ref, band_far, out_ref, pulses, band, sems):
    copies = []
    for level in range(LEVELS):
        span = slice(2 * level, 2 * level + 2)
        copies.append(pltpu.make_async_copy(band_far.at[span], band.at[span], sems.at[level]))
    for copy in copies:
        copy.start()
    me = me_ref[0]
    apart = comp_ref[...].astype(F32)
    for x in range(2):
        for part in range(2):
            for q in range(8):
                n = x * 8 + (((q & 3) * 2 + (q >> 2)) ^ me)
                blocks = []
                for c in range(CHAN):
                    at = (x * 8 + c) * SENT + (q >> 2) * 2 * CUT + part * CUT
                    blocks.append(apart[at : at + CUT, (q & 3) * 32 : (q & 3) * 32 + 32])
                pulses[part, n, :CUT, :] = jnp.concatenate(blocks, axis=1)
    pulse = jnp.concatenate(
        [pulses[part, n, :CUT, :] for part in range(2) for n in REVERSED], axis=0
    ).astype(BF)
    formed = dot(pulse, operator_ref[0]) + dot(pulse, operator_ref[1])
    real = formed[:COLS, :ANG] - formed[COLS:, ANG:]
    imag = formed[COLS:, :ANG] + formed[:COLS, ANG:]
    half = COLS // 2
    for level in range(LEVELS):
        block = COLS >> level
        sides = []
        for c in range(2):
            starts = [k * block + c * (block // 2) for k in range(1 << level)]
            sides.append(
                jnp.concatenate(
                    [part[at : at + block // 2] for part in (real, imag) for at in starts], axis=0
                )
            )
        left = jnp.concatenate(sides, axis=1)
        top = left.astype(BF)
        rest = (left - top.astype(F32)).astype(BF)
        reals, imags = [], []
        copies[level].wait()
        for h in range(2):
            weight = band[2 * level + h]
            out = dot(top, weight) + dot(rest, weight)
            reals.append(out[:half, :ANG] - out[half:, ANG:])
            imags.append(out[half:, :ANG] + out[:half, ANG:])
        real = jnp.concatenate(reals, axis=0)
        imag = jnp.concatenate(imags, axis=0)
    power = real * real + imag * imag
    rest = jnp.zeros((PAD - CUT, ANG), F32)
    for n in range(GROUP):
        out_ref[n] = jnp.concatenate([power[n * CUT : (n + 1) * CUT], rest], axis=0).astype(BF)


def despeckle_body(chan_ref, power_ref, rate_ref, out_ref, bins):
    for t in range(GROUP):
        at, count = (t * CUT, CUT) if t < 8 else (LOWER + (t - 8) * 8, 8)
        bins[at : at + count, :] = power_ref[t].astype(F32)[:count]
    current = bins[...]
    cell = iota((PICKED, ANG), 0) + (chan_ref[0] * 128 - HALO)
    inside = (cell >= 0) & (cell < 1024)
    rate = jnp.broadcast_to(rate_ref[...], (PICKED, ANG))
    for _ in range(PASSES):
        before = pltpu.roll(current, 1, 0)
        after = pltpu.roll(current, PICKED - 1, 0)
        current = jnp.where(inside, current + rate * (before - 2.0 * current + after), 0.0)
    out_ref[...] = current[HALO : HALO + 128, :].T


def doppler_table():
    index = np.arange(PULSES)
    phase = np.float32(2.0 * np.pi / PULSES) * (
        index[:, None] * index[None, :] % PULSES
    ).astype(np.float32)
    factor = np.float32(1.0 / np.sqrt(PULSES))
    parts = np.stack([np.cos(phase) * factor, -np.sin(phase) * factor])
    return parts.astype(ml_dtypes.bfloat16).astype(np.float32)


def flipped(value, axis, mask):
    pairs = [(source, source ^ mask) for source in range(lax.axis_size(axis))]
    return lax.ppermute(value, axis, pairs)


def exchange(value, axes):
    return lax.all_to_all(value, axes, split_axis=0, concat_axis=0, tiled=True)


def local(
    raw_pulses, range_filter, channel_mix, steer_angles, band_offsets, band_weights, smoothing
):
    raw = pl.pallas_call(
        raw_body,
        out_shape=jax.ShapeDtypeStruct((PULSES, 4096), BF),
        in_specs=[WHOLE],
        out_specs=WHOLE,
        compiler_params=params(8),
        name="raw_order",
    )(raw_pulses.reshape(2, PULSES, 2048))
    own = jnp.concatenate([raw] + [flipped(raw, "y", mask) for mask in (1, 2, 3)], axis=0)
    other = flipped(own, "core", 1)

    rows = pl.pallas_call(
        copies_body,
        out_shape=jax.ShapeDtypeStruct((16, 2, 4, 1024), BF),
        in_specs=[LEFT],
        out_specs=LEFT,
        scratch_shapes=[
            pltpu.VMEM((2, 4, 1024), BF),
            pltpu.SemaphoreType.DMA,
            pltpu.SemaphoreType.DMA((16,)),
        ],
        compiler_params=params(60),
        name="copies",
    )(range_filter)
    rows = exchange(rows, ALONG_Z)
    picked = pl.pallas_call(
        pick_body,
        out_shape=jax.ShapeDtypeStruct((4, ROW, PICKED, 128), BF),
        in_specs=[WHOLE],
        out_specs=LEFT,
        scratch_shapes=[
            pltpu.VMEM((128, 1024), F32),
            pltpu.VMEM((ROW, PICKED, 128), BF),
            pltpu.SemaphoreType.DMA((4, ROW)),
        ],
        compiler_params=params(8),
        name="pick_bins",
    )(rows)
    filters = exchange(picked.reshape(32, PICKED, 128), PLANE)

    weights = band_weights.reshape(LEVELS, 2, 2, 2, ANG, BAND).transpose(0, 3, 1, 2, 5, 4)
    band = pl.pallas_call(
        band_body,
        grid=(2 * LEVELS,),
        out_shape=jax.ShapeDtypeStruct((2 * LEVELS, 2 * ANG, 2 * ANG), BF),
        in_specs=[
            pl.BlockSpec((1, 1, ANG), lambda i: (i, 0, 0)),
            pl.BlockSpec((1, 2, 2, BAND, ANG), lambda i: (i, 0, 0, 0, 0)),
        ],
        out_specs=pl.BlockSpec((1, 2 * ANG, 2 * ANG), lambda i: (i, 0, 0)),
        compiler_params=params(4),
        name="band",
    )(
        band_offsets.reshape(2 * LEVELS, 1, ANG),
        weights.reshape(2 * LEVELS, 2, 2, BAND, ANG),
    )

    filters, band = lax.optimization_barrier((filters, band))
    compressed = pl.pallas_call(
        compress_body,
        out_shape=jax.ShapeDtypeStruct((GROUP, SENT, 128), BF),
        in_specs=[WHOLE] * 3,
        out_specs=WHOLE,
        scratch_shapes=[pltpu.VMEM((256, 4096), BF)],
        compiler_params=params(16),
        name="compress",
    )(filters, own, other)

    compressed, steer_angles, channel_mix = lax.optimization_barrier(
        (compressed, steer_angles, channel_mix)
    )
    offset = jnp.arange(ANG, dtype=jnp.int32).astype(F32) - 0.5 * ANG
    phase = steer_angles[None, :] * offset[:, None]
    factor = 1.0 / np.sqrt(ANG)
    beams = jnp.stack([jnp.cos(phase) * factor, jnp.sin(phase) * factor]).astype(BF)
    mix = channel_mix.transpose(0, 3, 2, 1).reshape(2, CHAN, 256)
    doppler = jnp.asarray(np.tile(doppler_table().transpose(0, 2, 1), (1, 1, CHAN)))
    operator = pl.pallas_call(
        operator_body,
        out_shape=jax.ShapeDtypeStruct((2, 256, 2 * ANG), BF),
        in_specs=[WHOLE] * 3,
        out_specs=WHOLE,
        compiler_params=params(8),
        name="operator",
    )(mix, doppler, beams)
    compressed = exchange(compressed, ("x0", "chan"))
    me = (lax.axis_index("y") * 2 + lax.axis_index("core")).astype(jnp.int32).reshape(1)
    power = pl.pallas_call(
        merge_body,
        out_shape=jax.ShapeDtypeStruct((GROUP, PAD, ANG), BF),
        in_specs=[SCALAR, WHOLE, WHOLE, LEFT],
        out_specs=WHOLE,
        scratch_shapes=[
            pltpu.VMEM((2, GROUP, PAD, 256), F32),
            pltpu.VMEM((2 * LEVELS, 2 * ANG, 2 * ANG), BF),
            pltpu.SemaphoreType.DMA((LEVELS,)),
        ],
        compiler_params=params(52),
        name="merge",
    )(me, compressed.reshape(GROUP * SENT, 128), operator, band)
    power = exchange(power, MERGE)
    chan = lax.axis_index("chan").astype(jnp.int32).reshape(1)
    return pl.pallas_call(
        despeckle_body,
        out_shape=jax.ShapeDtypeStruct((ANG, 128), F32),
        in_specs=[SCALAR] + [WHOLE] * 2,
        out_specs=WHOLE,
        scratch_shapes=[pltpu.VMEM((PICKED, ANG), F32)],
        compiler_params=params(4),
        name="despeckle",
    )(chan, power, smoothing.reshape(1, ANG))


def solution(mesh):
    split = Mesh(mesh.devices.reshape(2, 2, 2, 4, 2, mesh.shape["chan"]), AXES)
    placed = (
        P(None, SUB, "chan", None),
        P(None, AXES, None),
        P(),
        P(),
        P(),
        P(),
        P(SUB),
    )
    return jax.shard_map(
        local, mesh=split, in_specs=placed, out_specs=P(SUB, "chan"), check_vma=False
    )
```

```python
import functools

import jax
import jax.numpy as jnp
import ml_dtypes
import numpy as np
from jax import lax
from jax.experimental import pallas as pl
from jax.experimental.pallas import tpu as pltpu
from jax.sharding import Mesh
from jax.sharding import PartitionSpec as P

ANG = 256
BAND = 8
LEVELS = 4
PASSES = 3
PULSES = 32
CHAN = 8
GROUP = 16
ROW = 8
CUT = 9
PAD = 16
SENT = 40
HALO = 4
COLS = GROUP * CUT
LOWER = 8 * CUT
PICKED = LOWER + 64
REVERSED = [8 * (m & 1) + 4 * (m >> 1 & 1) + 2 * (m >> 2 & 1) + (m >> 3) for m in range(GROUP)]
AXES = ("zh", "x1", "x0", "y", "core", "chan")
SUB = ("zh", "x1", "x0", "y", "core")
ALONG_Z = ("zh", "chan")
PLANE = ("x1", "x0", "y", "core")
MERGE = ("x0", "y", "core")
BF = jnp.bfloat16
F32 = jnp.float32
WHOLE = pl.BlockSpec(memory_space=pltpu.VMEM)
LEFT = pl.BlockSpec(memory_space=pltpu.HBM)
SCALAR = pl.BlockSpec(memory_space=pltpu.SMEM)


def params(mib):
    return pltpu.CompilerParams(vmem_limit_bytes=mib << 20)


def iota(shape, dim):
    return lax.broadcasted_iota(jnp.int32, shape, dim)


def dot(left, right):
    return jnp.dot(left, right, preferred_element_type=F32)


def dot_t(left, right):
    return lax.dot_general(left, right, (((1,), (1,)), ((), ())), preferred_element_type=F32)


def raw_body(raw_ref, out_ref):
    row, col = iota((512, 512), 0), iota((512, 512), 1)
    quarter, part, half, k = col >> 7, (col >> 6) & 1, (col >> 5) & 1, col & 31
    source = part * 256 + half * 128 + quarter * 32 + k
    sign = jnp.where(part == 1, -1.0, 1.0)
    order = jnp.where(row == source, sign, 0.0).astype(BF)
    rows = []
    for u in range(8):
        rows.append(
            jnp.concatenate(
                [
                    raw_ref[part, :, half * 1024 + u * 128 : half * 1024 + (u + 1) * 128]
                    for part in range(2)
                    for half in range(2)
                ],
                axis=1,
            )
        )
    moved = dot(jnp.concatenate(rows, axis=0), order).astype(BF)
    for u in range(8):
        out_ref[:, u * 512 : (u + 1) * 512] = moved[u * 32 : (u + 1) * 32]


def copies_body(filter_far, out_far, rows, sem, sems):
    first = pltpu.make_async_copy(filter_far, rows, sem)
    first.start()
    first.wait()
    copies = [pltpu.make_async_copy(rows, out_far.at[z], sems.at[z]) for z in range(16)]
    for copy in copies:
        copy.start()
    for copy in copies:
        copy.wait()


def pick_body(filter_ref, out_far, ordered, picked, sems):
    for z in range(16):
        for part in range(2):
            at = part * 64 + z * 4
            ordered[at : at + 4, :] = filter_ref[z, part].astype(F32)
    rows = ordered[...].astype(BF)
    r, k = iota((LOWER, 1024), 0), iota((64, 1024), 0)
    dest = r // CUT
    lower = iota((LOWER, 1024), 1) - (128 * dest - HALO + r - dest * CUT)
    upper = iota((64, 1024), 1) - (128 * (k >> 3) - HALO + LOWER + (k & 7))
    copies = []
    for g in range(ROW):
        hits = [jnp.where(lower == CUT * g, 1.0, 0.0), jnp.where(upper == 8 * g, 1.0, 0.0)]
        pick = jnp.concatenate(hits, axis=0).astype(BF)
        picked[g] = dot_t(pick, rows).astype(BF)
        for x in range(4):
            copy = pltpu.make_async_copy(picked.at[g], out_far.at[x, g], sems.at[x, g])
            copy.start()
            copies.append(copy)
    for copy in copies:
        copy.wait()


def compress_body(filter_ref, own_ref, other_ref, out_ref, pulses):
    pulses[:128, :] = own_ref[...]
    pulses[128:, :] = other_ref[...]
    first, second = [], []
    for s in range(32):
        block = filter_ref[s]
        first.append(block)
        second.append(jnp.concatenate([block[:, 64:], -block[:, :64]], axis=1))
    left = jnp.concatenate(
        [jnp.concatenate(first, axis=1), jnp.concatenate(second, axis=1)], axis=0
    )
    summed = dot_t(left, pulses[...])
    row, col = iota((32 * GROUP, 2 * PICKED), 0), iota((32 * GROUP, 2 * PICKED), 1)
    within = row & 31
    j = jnp.where(within >= CUT, within - CUT, within)
    c = (row >> 5) & 7
    upper = row >= 8 * 32
    source = jnp.where(upper, LOWER + 8 * c, CUT * c) + j
    source = jnp.where(within >= CUT, source + PICKED, source)
    held = (within < 2 * CUT) & ((j < 8) | ~upper)
    order = jnp.where((col == source) & held, 1.0, 0.0).astype(BF)
    moved = dot(order, summed.astype(BF))
    rest = jnp.zeros((SENT - 4 * CUT, 128), F32)
    for dest in range(GROUP):
        block = moved[dest * 32 : dest * 32 + 2 * CUT]
        out_ref[dest] = jnp.concatenate([block[:, :128], block[:, 128:], rest], axis=0).astype(BF)


def operator_body(mix_ref, dop_ref, beam_ref, out_ref):
    real, imag = [], []
    for c in range(CHAN):
        mr, mi = mix_ref[0, c : c + 1, :], mix_ref[1, c : c + 1, :]
        real.append(mr * dop_ref[0] - mi * dop_ref[1])
        imag.append(mr * dop_ref[1] + mi * dop_ref[0])
    both = jnp.concatenate(real + imag, axis=0)
    top = both.astype(BF)
    rest = (both - top.astype(F32)).astype(BF)
    by_real = dot(top, beam_ref[0]) + dot(rest, beam_ref[0])
    by_imag = dot(top, beam_ref[1]) + dot(rest, beam_ref[1])
    whole = jnp.concatenate(
        [by_real[:256] - by_imag[256:], by_real[256:] + by_imag[:256]], axis=1
    )
    top = whole.astype(BF)
    out_ref[0] = top
    out_ref[1] = (whole - top.astype(F32)).astype(BF)


def band_body(offset_ref, weight_ref, out_ref):
    strip = 32
    offset = jnp.broadcast_to(offset_ref[0], (strip, ANG))
    for start in range(0, ANG, strip):
        step = iota((strip, ANG), 0) + start - offset
        hits = [step == j for j in range(BAND)]
        for c in range(2):
            for part in range(2):
                value = jnp.zeros((strip, ANG), F32)
                for j in range(BAND):
                    value = jnp.where(hits[j], weight_ref[0, c, part, j : j + 1, :], value)
                rows = slice(c * ANG + start, c * ANG + start + strip)
                lanes = slice(part * ANG, (part + 1) * ANG)
                top = value.astype(BF)
                out_ref[0, 0, rows, lanes] = top
                out_ref[0, 1, rows, lanes] = (value - top.astype(F32)).astype(BF)


def merge_body(me_ref, comp_ref, operator_ref, band_far, out_ref, pulses, band, sems):
    copies = []
    for level in range(LEVELS):
        span = slice(2 * level, 2 * level + 2)
        copies.append(pltpu.make_async_copy(band_far.at[span], band.at[span], sems.at[level]))
    for copy in copies:
        copy.start()
    me = me_ref[0]
    apart = comp_ref[...].astype(F32)
    for x in range(2):
        for part in range(2):
            for q in range(8):
                n = x * 8 + (((q & 3) * 2 + (q >> 2)) ^ me)
                blocks = []
                for c in range(CHAN):
                    at = (x * 8 + c) * SENT + (q >> 2) * 2 * CUT + part * CUT
                    blocks.append(apart[at : at + CUT, (q & 3) * 32 : (q & 3) * 32 + 32])
                pulses[part, n, :CUT, :] = jnp.concatenate(blocks, axis=1)
    pulse = jnp.concatenate(
        [pulses[part, n, :CUT, :] for part in range(2) for n in REVERSED], axis=0
    ).astype(BF)
    formed = dot(pulse, operator_ref[0]) + dot(pulse, operator_ref[1])
    real = formed[:COLS, :ANG] - formed[COLS:, ANG:]
    imag = formed[COLS:, :ANG] + formed[:COLS, ANG:]
    half = COLS // 2
    for level in range(LEVELS):
        block = COLS >> level
        sides = []
        for c in range(2):
            starts = [k * block + c * (block // 2) for k in range(1 << level)]
            sides.append(
                jnp.concatenate(
                    [part[at : at + block // 2] for part in (real, imag) for at in starts], axis=0
                )
            )
        left = jnp.concatenate(sides, axis=1)
        top = left.astype(BF)
        rest = (left - top.astype(F32)).astype(BF)
        reals, imags = [], []
        copies[level].wait()
        for h in range(2):
            weight = band[2 * level + h, 0]
            out = dot(top, weight) + dot(rest, weight) + dot(top, band[2 * level + h, 1])
            reals.append(out[:half, :ANG] - out[half:, ANG:])
            imags.append(out[half:, :ANG] + out[:half, ANG:])
        real = jnp.concatenate(reals, axis=0)
        imag = jnp.concatenate(imags, axis=0)
    power = real * real + imag * imag
    rest = jnp.zeros((PAD - CUT, ANG), F32)
    for n in range(GROUP):
        out_ref[n] = jnp.concatenate([power[n * CUT : (n + 1) * CUT], rest], axis=0).astype(BF)


def despeckle_body(chan_ref, power_ref, rate_ref, out_ref, bins):
    for t in range(GROUP):
        at, count = (t * CUT, CUT) if t < 8 else (LOWER + (t - 8) * 8, 8)
        bins[at : at + count, :] = power_ref[t].astype(F32)[:count]
    current = bins[...]
    cell = iota((PICKED, ANG), 0) + (chan_ref[0] * 128 - HALO)
    inside = (cell >= 0) & (cell < 1024)
    rate = jnp.broadcast_to(rate_ref[...], (PICKED, ANG))
    for _ in range(PASSES):
        before = pltpu.roll(current, 1, 0)
        after = pltpu.roll(current, PICKED - 1, 0)
        current = jnp.where(inside, current + rate * (before - 2.0 * current + after), 0.0)
    out_ref[...] = current[HALO : HALO + 128, :].T


def doppler_table():
    index = np.arange(PULSES)
    phase = np.float32(2.0 * np.pi / PULSES) * (
        index[:, None] * index[None, :] % PULSES
    ).astype(np.float32)
    factor = np.float32(1.0 / np.sqrt(PULSES))
    parts = np.stack([np.cos(phase) * factor, -np.sin(phase) * factor])
    return parts.astype(ml_dtypes.bfloat16).astype(np.float32)


def flipped(value, axis, mask):
    pairs = [(source, source ^ mask) for source in range(lax.axis_size(axis))]
    return lax.ppermute(value, axis, pairs)


def exchange(value, axes):
    return lax.all_to_all(value, axes, split_axis=0, concat_axis=0, tiled=True)


def local(
    raw_pulses, range_filter, channel_mix, steer_angles, band_offsets, band_weights, smoothing
):
    raw = pl.pallas_call(
        raw_body,
        out_shape=jax.ShapeDtypeStruct((PULSES, 4096), BF),
        in_specs=[WHOLE],
        out_specs=WHOLE,
        compiler_params=params(8),
        name="raw_order",
    )(raw_pulses.reshape(2, PULSES, 2048))
    own = jnp.concatenate([raw] + [flipped(raw, "y", mask) for mask in (1, 2, 3)], axis=0)
    other = flipped(own, "core", 1)

    rows = pl.pallas_call(
        copies_body,
        out_shape=jax.ShapeDtypeStruct((16, 2, 4, 1024), BF),
        in_specs=[LEFT],
        out_specs=LEFT,
        scratch_shapes=[
            pltpu.VMEM((2, 4, 1024), BF),
            pltpu.SemaphoreType.DMA,
            pltpu.SemaphoreType.DMA((16,)),
        ],
        compiler_params=params(60),
        name="copies",
    )(range_filter)
    rows = exchange(rows, ALONG_Z)
    picked = pl.pallas_call(
        pick_body,
        out_shape=jax.ShapeDtypeStruct((4, ROW, PICKED, 128), BF),
        in_specs=[WHOLE],
        out_specs=LEFT,
        scratch_shapes=[
            pltpu.VMEM((128, 1024), F32),
            pltpu.VMEM((ROW, PICKED, 128), BF),
            pltpu.SemaphoreType.DMA((4, ROW)),
        ],
        compiler_params=params(8),
        name="pick_bins",
    )(rows)
    filters = exchange(picked.reshape(32, PICKED, 128), PLANE)

    weights = band_weights.reshape(LEVELS, 2, 2, 2, ANG, BAND).transpose(0, 3, 1, 2, 5, 4)
    band = pl.pallas_call(
        band_body,
        grid=(2 * LEVELS,),
        out_shape=jax.ShapeDtypeStruct((2 * LEVELS, 2, 2 * ANG, 2 * ANG), BF),
        in_specs=[
            pl.BlockSpec((1, 1, ANG), lambda i: (i, 0, 0)),
            pl.BlockSpec((1, 2, 2, BAND, ANG), lambda i: (i, 0, 0, 0, 0)),
        ],
        out_specs=pl.BlockSpec((1, 2, 2 * ANG, 2 * ANG), lambda i: (i, 0, 0, 0)),
        compiler_params=params(6),
        name="band",
    )(
        band_offsets.reshape(2 * LEVELS, 1, ANG),
        weights.reshape(2 * LEVELS, 2, 2, BAND, ANG),
    )

    filters, band = lax.optimization_barrier((filters, band))
    compressed = pl.pallas_call(
        compress_body,
        out_shape=jax.ShapeDtypeStruct((GROUP, SENT, 128), BF),
        in_specs=[WHOLE] * 3,
        out_specs=WHOLE,
        scratch_shapes=[pltpu.VMEM((256, 4096), BF)],
        compiler_params=params(16),
        name="compress",
    )(filters, own, other)

    compressed, steer_angles, channel_mix = lax.optimization_barrier(
        (compressed, steer_angles, channel_mix)
    )
    offset = jnp.arange(ANG, dtype=jnp.int32).astype(F32) - 0.5 * ANG
    phase = steer_angles[None, :] * offset[:, None]
    factor = 1.0 / np.sqrt(ANG)
    beams = jnp.stack([jnp.cos(phase) * factor, jnp.sin(phase) * factor]).astype(BF)
    mix = channel_mix.transpose(0, 3, 2, 1).reshape(2, CHAN, 256)
    doppler = jnp.asarray(np.tile(doppler_table().transpose(0, 2, 1), (1, 1, CHAN)))
    operator = pl.pallas_call(
        operator_body,
        out_shape=jax.ShapeDtypeStruct((2, 256, 2 * ANG), BF),
        in_specs=[WHOLE] * 3,
        out_specs=WHOLE,
        compiler_params=params(8),
        name="operator",
    )(mix, doppler, beams)
    compressed = exchange(compressed, ("x0", "chan"))
    me = (lax.axis_index("y") * 2 + lax.axis_index("core")).astype(jnp.int32).reshape(1)
    power = pl.pallas_call(
        merge_body,
        out_shape=jax.ShapeDtypeStruct((GROUP, PAD, ANG), BF),
        in_specs=[SCALAR, WHOLE, WHOLE, LEFT],
        out_specs=WHOLE,
        scratch_shapes=[
            pltpu.VMEM((2, GROUP, PAD, 256), F32),
            pltpu.VMEM((2 * LEVELS, 2, 2 * ANG, 2 * ANG), BF),
            pltpu.SemaphoreType.DMA((LEVELS,)),
        ],
        compiler_params=params(52),
        name="merge",
    )(me, compressed.reshape(GROUP * SENT, 128), operator, band)
    power = exchange(power, MERGE)
    chan = lax.axis_index("chan").astype(jnp.int32).reshape(1)
    return pl.pallas_call(
        despeckle_body,
        out_shape=jax.ShapeDtypeStruct((ANG, 128), F32),
        in_specs=[SCALAR] + [WHOLE] * 2,
        out_specs=WHOLE,
        scratch_shapes=[pltpu.VMEM((PICKED, ANG), F32)],
        compiler_params=params(4),
        name="despeckle",
    )(chan, power, smoothing.reshape(1, ANG))


def solution(mesh):
    split = Mesh(mesh.devices.reshape(2, 2, 2, 4, 2, mesh.shape["chan"]), AXES)
    placed = (
        P(None, SUB, "chan", None),
        P(None, AXES, None),
        P(),
        P(),
        P(),
        P(),
        P(SUB),
    )
    return jax.shard_map(
        local, mesh=split, in_specs=placed, out_specs=P(SUB, "chan"), check_vma=False
    )
```

```python
import functools

import jax
import jax.numpy as jnp
import ml_dtypes
import numpy as np
from jax import lax
from jax.experimental import pallas as pl
from jax.experimental.pallas import tpu as pltpu
from jax.sharding import Mesh
from jax.sharding import PartitionSpec as P

ANG = 256
BAND = 8
LEVELS = 4
PASSES = 3
PULSES = 32
CHAN = 8
GROUP = 16
ROW = 8
CUT = 9
PAD = 16
SENT = 40
HALO = 4
COLS = GROUP * CUT
LOWER = 8 * CUT
PICKED = LOWER + 64
REVERSED = [8 * (m & 1) + 4 * (m >> 1 & 1) + 2 * (m >> 2 & 1) + (m >> 3) for m in range(GROUP)]
AXES = ("zh", "x1", "x0", "y", "core", "chan")
SUB = ("zh", "x1", "x0", "y", "core")
ALONG_Z = ("zh", "chan")
PLANE = ("x1", "x0", "y", "core")
MERGE = ("x0", "y", "core")
BF = jnp.bfloat16
F32 = jnp.float32
WHOLE = pl.BlockSpec(memory_space=pltpu.VMEM)
LEFT = pl.BlockSpec(memory_space=pltpu.HBM)
SCALAR = pl.BlockSpec(memory_space=pltpu.SMEM)


def params(mib):
    return pltpu.CompilerParams(vmem_limit_bytes=mib << 20)


def iota(shape, dim):
    return lax.broadcasted_iota(jnp.int32, shape, dim)


def dot(left, right):
    return jnp.dot(left, right, preferred_element_type=F32)


def dot_t(left, right):
    return lax.dot_general(left, right, (((1,), (1,)), ((), ())), preferred_element_type=F32)


def raw_body(raw_ref, out_ref):
    row, col = iota((512, 512), 0), iota((512, 512), 1)
    quarter, part, half, k = col >> 7, (col >> 6) & 1, (col >> 5) & 1, col & 31
    source = part * 256 + half * 128 + quarter * 32 + k
    sign = jnp.where(part == 1, -1.0, 1.0)
    order = jnp.where(row == source, sign, 0.0).astype(BF)
    rows = []
    for u in range(8):
        rows.append(
            jnp.concatenate(
                [
                    raw_ref[part, :, half * 1024 + u * 128 : half * 1024 + (u + 1) * 128]
                    for part in range(2)
                    for half in range(2)
                ],
                axis=1,
            )
        )
    moved = dot(jnp.concatenate(rows, axis=0), order).astype(BF)
    for u in range(8):
        out_ref[:, u * 512 : (u + 1) * 512] = moved[u * 32 : (u + 1) * 32]


def copies_body(filter_far, out_far, rows, sem, sems):
    first = pltpu.make_async_copy(filter_far, rows, sem)
    first.start()
    first.wait()
    copies = [pltpu.make_async_copy(rows, out_far.at[z], sems.at[z]) for z in range(16)]
    for copy in copies:
        copy.start()
    for copy in copies:
        copy.wait()


def pick_body(filter_ref, out_far, ordered, picked, sems):
    for z in range(16):
        for part in range(2):
            at = part * 64 + z * 4
            ordered[at : at + 4, :] = filter_ref[z, part].astype(F32)
    rows = ordered[...].astype(BF)
    r, k = iota((LOWER, 1024), 0), iota((64, 1024), 0)
    dest = r // CUT
    lower = iota((LOWER, 1024), 1) - (128 * dest - HALO + r - dest * CUT)
    upper = iota((64, 1024), 1) - (128 * (k >> 3) - HALO + LOWER + (k & 7))
    copies = []
    for g in range(ROW):
        hits = [jnp.where(lower == CUT * g, 1.0, 0.0), jnp.where(upper == 8 * g, 1.0, 0.0)]
        pick = jnp.concatenate(hits, axis=0).astype(BF)
        picked[g] = dot_t(pick, rows).astype(BF)
        for x in range(4):
            copy = pltpu.make_async_copy(picked.at[g], out_far.at[x, g], sems.at[x, g])
            copy.start()
            copies.append(copy)
    for copy in copies:
        copy.wait()


def compress_body(filter_ref, own_ref, other_ref, out_ref, pulses):
    pulses[:128, :] = own_ref[...]
    pulses[128:, :] = other_ref[...]
    first, second = [], []
    for s in range(32):
        block = filter_ref[s]
        first.append(block)
        second.append(jnp.concatenate([block[:, 64:], -block[:, :64]], axis=1))
    left = jnp.concatenate(
        [jnp.concatenate(first, axis=1), jnp.concatenate(second, axis=1)], axis=0
    )
    summed = dot_t(left, pulses[...])
    row, col = iota((32 * GROUP, 2 * PICKED), 0), iota((32 * GROUP, 2 * PICKED), 1)
    within = row & 31
    j = jnp.where(within >= CUT, within - CUT, within)
    c = (row >> 5) & 7
    upper = row >= 8 * 32
    source = jnp.where(upper, LOWER + 8 * c, CUT * c) + j
    source = jnp.where(within >= CUT, source + PICKED, source)
    held = (within < 2 * CUT) & ((j < 8) | ~upper)
    order = jnp.where((col == source) & held, 1.0, 0.0).astype(BF)
    moved = dot(order, summed.astype(BF))
    rest = jnp.zeros((SENT - 4 * CUT, 128), F32)
    for dest in range(GROUP):
        block = moved[dest * 32 : dest * 32 + 2 * CUT]
        out_ref[dest] = jnp.concatenate([block[:, :128], block[:, 128:], rest], axis=0).astype(BF)


def operator_body(mix_ref, dop_ref, beam_ref, out_ref):
    real, imag = [], []
    for c in range(CHAN):
        mr, mi = mix_ref[0, c : c + 1, :], mix_ref[1, c : c + 1, :]
        real.append(mr * dop_ref[0] - mi * dop_ref[1])
        imag.append(mr * dop_ref[1] + mi * dop_ref[0])
    both = jnp.concatenate(real + imag, axis=0)
    top = both.astype(BF)
    rest = (both - top.astype(F32)).astype(BF)
    by_real = dot(top, beam_ref[0]) + dot(rest, beam_ref[0])
    by_imag = dot(top, beam_ref[1]) + dot(rest, beam_ref[1])
    whole = jnp.concatenate(
        [by_real[:256] - by_imag[256:], by_real[256:] + by_imag[:256]], axis=1
    )
    top = whole.astype(BF)
    out_ref[0] = top
    out_ref[1] = (whole - top.astype(F32)).astype(BF)


def band_body(offset_ref, weight_ref, out_ref):
    strip = 32
    offset = jnp.broadcast_to(offset_ref[0], (strip, ANG))
    for start in range(0, ANG, strip):
        step = iota((strip, ANG), 0) + start - offset
        hits = [step == j for j in range(BAND)]
        for c in range(2):
            for part in range(2):
                value = jnp.zeros((strip, ANG), F32)
                for j in range(BAND):
                    value = jnp.where(hits[j], weight_ref[0, c, part, j : j + 1, :], value)
                rows = slice(c * ANG + start, c * ANG + start + strip)
                lanes = slice(part * ANG, (part + 1) * ANG)
                top = value.astype(BF)
                out_ref[0, 0, rows, lanes] = top
                out_ref[0, 1, rows, lanes] = (value - top.astype(F32)).astype(BF)


def merge_body(me_ref, comp_ref, operator_ref, band_far, out_ref, pulses, band, sems):
    copies = []
    for k in range(2 * LEVELS):
        copies.append(pltpu.make_async_copy(band_far.at[k], band.at[k], sems.at[k]))
    for copy in copies:
        copy.start()
    me = me_ref[0]
    apart = comp_ref[...].astype(F32)
    for x in range(2):
        for part in range(2):
            for q in range(8):
                n = x * 8 + (((q & 3) * 2 + (q >> 2)) ^ me)
                blocks = []
                for c in range(CHAN):
                    at = (x * 8 + c) * SENT + (q >> 2) * 2 * CUT + part * CUT
                    blocks.append(apart[at : at + CUT, (q & 3) * 32 : (q & 3) * 32 + 32])
                pulses[part, n, :CUT, :] = jnp.concatenate(blocks, axis=1)
    pulse = jnp.concatenate(
        [pulses[part, n, :CUT, :] for part in range(2) for n in REVERSED], axis=0
    ).astype(BF)
    formed = dot(pulse, operator_ref[0]) + dot(pulse, operator_ref[1])
    real = formed[:COLS, :ANG] - formed[COLS:, ANG:]
    imag = formed[COLS:, :ANG] + formed[:COLS, ANG:]
    half = COLS // 2
    for level in range(LEVELS):
        block = COLS >> level
        sides = []
        for c in range(2):
            starts = [k * block + c * (block // 2) for k in range(1 << level)]
            sides.append(
                jnp.concatenate(
                    [part[at : at + block // 2] for part in (real, imag) for at in starts], axis=0
                )
            )
        left = jnp.concatenate(sides, axis=1)
        top = left.astype(BF)
        rest = (left - top.astype(F32)).astype(BF)
        reals, imags = [], []
        for h in range(2):
            copies[2 * level + h].wait()
            weight = band[2 * level + h, 0]
            out = dot(top, weight) + dot(rest, weight) + dot(top, band[2 * level + h, 1])
            reals.append(out[:half, :ANG] - out[half:, ANG:])
            imags.append(out[half:, :ANG] + out[:half, ANG:])
        real = jnp.concatenate(reals, axis=0)
        imag = jnp.concatenate(imags, axis=0)
    power = real * real + imag * imag
    rest = jnp.zeros((PAD - CUT, ANG), F32)
    for n in range(GROUP):
        out_ref[n] = jnp.concatenate([power[n * CUT : (n + 1) * CUT], rest], axis=0).astype(BF)


def despeckle_body(chan_ref, power_ref, rate_ref, out_ref, bins):
    for t in range(GROUP):
        at, count = (t * CUT, CUT) if t < 8 else (LOWER + (t - 8) * 8, 8)
        bins[at : at + count, :] = power_ref[t].astype(F32)[:count]
    current = bins[...]
    cell = iota((PICKED, ANG), 0) + (chan_ref[0] * 128 - HALO)
    inside = (cell >= 0) & (cell < 1024)
    rate = jnp.broadcast_to(rate_ref[...], (PICKED, ANG))
    for _ in range(PASSES):
        before = pltpu.roll(current, 1, 0)
        after = pltpu.roll(current, PICKED - 1, 0)
        current = jnp.where(inside, current + rate * (before - 2.0 * current + after), 0.0)
    out_ref[...] = current[HALO : HALO + 128, :].T


def doppler_table():
    index = np.arange(PULSES)
    phase = np.float32(2.0 * np.pi / PULSES) * (
        index[:, None] * index[None, :] % PULSES
    ).astype(np.float32)
    factor = np.float32(1.0 / np.sqrt(PULSES))
    parts = np.stack([np.cos(phase) * factor, -np.sin(phase) * factor])
    return parts.astype(ml_dtypes.bfloat16).astype(np.float32)


def flipped(value, axis, mask):
    pairs = [(source, source ^ mask) for source in range(lax.axis_size(axis))]
    return lax.ppermute(value, axis, pairs)


def exchange(value, axes):
    return lax.all_to_all(value, axes, split_axis=0, concat_axis=0, tiled=True)


def local(
    raw_pulses, range_filter, channel_mix, steer_angles, band_offsets, band_weights, smoothing
):
    raw = pl.pallas_call(
        raw_body,
        out_shape=jax.ShapeDtypeStruct((PULSES, 4096), BF),
        in_specs=[WHOLE],
        out_specs=WHOLE,
        compiler_params=params(8),
        name="raw_order",
    )(raw_pulses.reshape(2, PULSES, 2048))
    own = jnp.concatenate([raw] + [flipped(raw, "y", mask) for mask in (1, 2, 3)], axis=0)
    other = flipped(own, "core", 1)

    rows = pl.pallas_call(
        copies_body,
        out_shape=jax.ShapeDtypeStruct((16, 2, 4, 1024), BF),
        in_specs=[LEFT],
        out_specs=LEFT,
        scratch_shapes=[
            pltpu.VMEM((2, 4, 1024), BF),
            pltpu.SemaphoreType.DMA,
            pltpu.SemaphoreType.DMA((16,)),
        ],
        compiler_params=params(60),
        name="copies",
    )(range_filter)
    rows = exchange(rows, ALONG_Z)
    picked = pl.pallas_call(
        pick_body,
        out_shape=jax.ShapeDtypeStruct((4, ROW, PICKED, 128), BF),
        in_specs=[WHOLE],
        out_specs=LEFT,
        scratch_shapes=[
            pltpu.VMEM((128, 1024), F32),
            pltpu.VMEM((ROW, PICKED, 128), BF),
            pltpu.SemaphoreType.DMA((4, ROW)),
        ],
        compiler_params=params(8),
        name="pick_bins",
    )(rows)
    filters = exchange(picked.reshape(32, PICKED, 128), PLANE)

    weights = band_weights.reshape(LEVELS, 2, 2, 2, ANG, BAND).transpose(0, 3, 1, 2, 5, 4)
    band = pl.pallas_call(
        band_body,
        grid=(2 * LEVELS,),
        out_shape=jax.ShapeDtypeStruct((2 * LEVELS, 2, 2 * ANG, 2 * ANG), BF),
        in_specs=[
            pl.BlockSpec((1, 1, ANG), lambda i: (i, 0, 0)),
            pl.BlockSpec((1, 2, 2, BAND, ANG), lambda i: (i, 0, 0, 0, 0)),
        ],
        out_specs=pl.BlockSpec((1, 2, 2 * ANG, 2 * ANG), lambda i: (i, 0, 0, 0)),
        compiler_params=params(6),
        name="band",
    )(
        band_offsets.reshape(2 * LEVELS, 1, ANG),
        weights.reshape(2 * LEVELS, 2, 2, BAND, ANG),
    )

    filters, band = lax.optimization_barrier((filters, band))
    compressed = pl.pallas_call(
        compress_body,
        out_shape=jax.ShapeDtypeStruct((GROUP, SENT, 128), BF),
        in_specs=[WHOLE] * 3,
        out_specs=WHOLE,
        scratch_shapes=[pltpu.VMEM((256, 4096), BF)],
        compiler_params=params(16),
        name="compress",
    )(filters, own, other)

    compressed, steer_angles, channel_mix = lax.optimization_barrier(
        (compressed, steer_angles, channel_mix)
    )
    offset = jnp.arange(ANG, dtype=jnp.int32).astype(F32) - 0.5 * ANG
    phase = steer_angles[None, :] * offset[:, None]
    factor = 1.0 / np.sqrt(ANG)
    beams = jnp.stack([jnp.cos(phase) * factor, jnp.sin(phase) * factor]).astype(BF)
    mix = channel_mix.transpose(0, 3, 2, 1).reshape(2, CHAN, 256)
    doppler = jnp.asarray(np.tile(doppler_table().transpose(0, 2, 1), (1, 1, CHAN)))
    operator = pl.pallas_call(
        operator_body,
        out_shape=jax.ShapeDtypeStruct((2, 256, 2 * ANG), BF),
        in_specs=[WHOLE] * 3,
        out_specs=WHOLE,
        compiler_params=params(8),
        name="operator",
    )(mix, doppler, beams)
    compressed = exchange(compressed, ("x0", "chan"))
    me = (lax.axis_index("y") * 2 + lax.axis_index("core")).astype(jnp.int32).reshape(1)
    power = pl.pallas_call(
        merge_body,
        out_shape=jax.ShapeDtypeStruct((GROUP, PAD, ANG), BF),
        in_specs=[SCALAR, WHOLE, WHOLE, LEFT],
        out_specs=WHOLE,
        scratch_shapes=[
            pltpu.VMEM((2, GROUP, PAD, 256), F32),
            pltpu.VMEM((2 * LEVELS, 2, 2 * ANG, 2 * ANG), BF),
            pltpu.SemaphoreType.DMA((2 * LEVELS,)),
        ],
        compiler_params=params(52),
        name="merge",
    )(me, compressed.reshape(GROUP * SENT, 128), operator, band)
    power = exchange(power, MERGE)
    chan = lax.axis_index("chan").astype(jnp.int32).reshape(1)
    return pl.pallas_call(
        despeckle_body,
        out_shape=jax.ShapeDtypeStruct((ANG, 128), F32),
        in_specs=[SCALAR] + [WHOLE] * 2,
        out_specs=WHOLE,
        scratch_shapes=[pltpu.VMEM((PICKED, ANG), F32)],
        compiler_params=params(4),
        name="despeckle",
    )(chan, power, smoothing.reshape(1, ANG))


def solution(mesh):
    split = Mesh(mesh.devices.reshape(2, 2, 2, 4, 2, mesh.shape["chan"]), AXES)
    placed = (
        P(None, SUB, "chan", None),
        P(None, AXES, None),
        P(),
        P(),
        P(),
        P(),
        P(SUB),
    )
    return jax.shard_map(
        local, mesh=split, in_specs=placed, out_specs=P(SUB, "chan"), check_vma=False
    )
```
